32 devices in a mesh: dp: 8 (over z, x), ctx: 4 (over y, core).
Axes of the slice: x: 2, y: 2, z: 4, core: 2. Of those that a mesh axis runs over, the one named last changes fastest.
Arguments:
- hidden_in: bfloat16 [4096, 8192], P(('dp', 'ctx')), may hold values from -6 to 6
- queries: bfloat16 [4096, 4096], P(('dp', 'ctx')), may hold values from -6 to 6
- keys: bfloat16 [4096, 512], P(('dp', 'ctx')), may hold values from -6 to 6
- values: bfloat16 [4096, 512], P(('dp', 'ctx')), may hold values from -6 to 6
- output_gradient: bfloat16 [4096, 4096], P(('dp', 'ctx')), may hold values from -6 to 6
- document_index: int32 [8, 512], P('dp', 'ctx'), may hold values from 0 to 7, never falling along the last dimension, each value on 1 to 256 neighbouring positions
Outputs:
- grad_queries: bfloat16 [4096, 4096], P(('dp', 'ctx'))
- key_gradient: bfloat16 [4096, 512], P(('dp', 'ctx'))
- value_gradient: bfloat16 [4096, 512], P(('dp', 'ctx'))
- value_weight_grad: float32 [8192, 512], P(('dp', 'ctx'))
The draws below stay inside these ranges and needn't reach their ends.
Inputs may be any that keep to these rules, and one draw needn't show every extreme that they name: `document_index`: never falling along a rollout; each document holds 1 to 256 tokens, one exactly 256.
All inputs are finite; a program needn't handle non-finite values.
Results may differ from the reference program's by a relative error of at most 0.0051.
Values may be sent and summed in bfloat16 or wider, within the bound.
A program may use at most 128 MiB of HBM per device.

```python
import math
import jax
import jax.numpy as jnp
import numpy as np
from jax import lax

D = 8192
QUERY_HEADS = 32
KEY_VALUE_HEADS = 4
HEAD_SIZE = 128
DOCS = 8
ROLLOUT_COUNT = 8
ROLLOUT_LENGTH = 512
TOKEN_COUNT = 4096
GROUP_QUERIES = 8


def draw_queries(key, part):
    final_result = jnp.clip(jax.random.normal(jax.random.fold_in(key, 22), (TOKEN_COUNT, QUERY_HEADS, HEAD_SIZE), jnp.float32), -6.0, 6.0)
    return final_result.reshape(TOKEN_COUNT, QUERY_HEADS * HEAD_SIZE).astype(jnp.bfloat16)


def draw_keys(key, part):
    final_result = jnp.clip(jax.random.normal(jax.random.fold_in(key, 32), (TOKEN_COUNT, KEY_VALUE_HEADS, HEAD_SIZE), jnp.float32), -6.0, 6.0)
    return final_result.reshape(TOKEN_COUNT, KEY_VALUE_HEADS * HEAD_SIZE).astype(jnp.bfloat16)


def with_spikes(values, own_key, source, target, blocks, factor):
    owner, partner = [(jnp.arange(values.shape[axis_at]) // (values.shape[axis_at] // blocks)).reshape([-1 if axis == axis_at else 1 for axis in range(values.ndim)]) for axis_at in (source, target)]
    chosen = jax.random.permutation(own_key, blocks)[partner]
    strong = (owner == chosen) | (owner == (partner + blocks // 2) % blocks)
    return jnp.where(strong, factor * values, values)


def levels(rng, shape, pieces, least, high):
    def one(dim, blocks):
        steps = jax.random.uniform(jax.random.fold_in(jax.random.fold_in(rng, 6), dim), (blocks,), jnp.float32, least / len(pieces), high / len(pieces))
        return jnp.repeat(jnp.exp(steps), shape[dim] // blocks).reshape((-1,) + (1,) * (len(shape) - dim - 1))

    loudness = one(*pieces[0])
    for cut in pieces[1:]:
        loudness = loudness * one(*cut)
    return loudness


def profile(number_of, total, bound, slope):
    loads = [(1 << 20) // math.isqrt(standing ** slope) + 1 for standing in range(2, number_of + 1)]
    spare, holding = total - bound - (number_of - 1), [1] * (number_of - 1)
    while spare > 0:
        candidates = [i for i in range(number_of - 1) if holding[i] < bound]
        pool, left = sum([loads[i] for i in candidates]), spare
        for i in candidates:
            extra = min(bound - holding[i], max(1, left * loads[i] // pool), spare)
            holding[i] = holding[i] + extra
            spare = spare - extra
    return np.array([bound] + holding)


def ragged(own_key, count, total, most, skew):
    if count == 2:
        one = jax.random.randint(own_key, (), max(1, total - most), min(most, total - 1) + 1)
        return jnp.stack([one, total - one])
    tallies = jnp.asarray(profile(count, total, most, skew), jnp.int32)
    twos = (count - 1) // 2
    giver, sink = tallies[1:1 + 2 * twos:2], tallies[2:2 + 2 * twos:2]
    room = jnp.minimum(giver - 1, most - sink)
    moved = jax.random.randint(jax.random.fold_in(own_key, 1), (twos,), 0, 1 << 20) % (room + 1)
    tallies = tallies.at[1:1 + 2 * twos:2].set(giver - moved).at[2:2 + 2 * twos:2].set(sink + moved)
    return tallies[jax.random.permutation(jax.random.fold_in(own_key, 2), count)]


def gaussian(own_key, dims, deviation, limit, shards=(), held_as=jnp.bfloat16):
    level = levels(own_key, dims, shards, -0.22, 0.18) if shards else 1.0
    result = jax.random.normal(own_key, dims, jnp.float32) * deviation * level
    return jnp.minimum(jnp.maximum(result, -limit), limit).astype(held_as)


def bell_draw_with(key, extent, scale, limit, pieces, heavy, held_as=jnp.bfloat16):
    values = scale * jax.random.normal(key, extent, jnp.float32)
    if pieces:
        values = values * levels(key, extent, pieces, -0.22, 0.18)
    return jnp.clip(with_spikes(values, jax.random.fold_in(key, 3), *heavy), -limit, limit).astype(held_as)


def setup_inputs(seed: int = 0) -> dict:
    streams_of = jax.random.split(jax.random.key(seed), 7)
    return {
        "hidden_in": bell_draw_with(streams_of[0], (TOKEN_COUNT, D), 1.0, 6.0, ((0, 32),), (0, 1, 32, 2.75)),
        "queries": draw_queries(jax.random.fold_in(streams_of[6], 71), 0),
        "keys": draw_keys(jax.random.fold_in(streams_of[6], 71), 0),
        "values": gaussian(streams_of[3], (TOKEN_COUNT, KEY_VALUE_HEADS * HEAD_SIZE), 1.0, 6.0, ((0, 32),)),
        "output_gradient": gaussian(streams_of[4], (TOKEN_COUNT, QUERY_HEADS * HEAD_SIZE), 1.0, 6.0, ((0, 32),)),
        "document_index": jax.vmap(lambda own: jnp.searchsorted(jnp.cumsum(ragged(own, DOCS, ROLLOUT_LENGTH, ROLLOUT_LENGTH // 2, 2)), jnp.arange(ROLLOUT_LENGTH), side="right"))(jax.random.split(streams_of[5], ROLLOUT_COUNT)).reshape((ROLLOUT_COUNT, ROLLOUT_LENGTH)).astype(jnp.int32),
    }


def group_grads(query_grp, key_head, value_head, grad_grp, doc_ids):
    inv_root = 1.0 / math.sqrt(HEAD_SIZE)
    positions = jnp.arange(ROLLOUT_LENGTH, dtype=jnp.int32)
    allowed = (positions[None, :] <= positions[:, None]) & (doc_ids[None, :] == doc_ids[:, None])
    scores = jnp.einsum('qhd,kd->hqk', query_grp, key_head) * inv_root
    scores = jnp.where(allowed[None], scores, -jnp.inf)
    row_max = lax.optimization_barrier(jnp.max(scores, axis=-1, keepdims=True))
    shifted = jnp.where(allowed[None], jnp.exp(scores - row_max), 0.0)
    attn_probs = shifted / lax.optimization_barrier(jnp.sum(shifted, axis=-1, keepdims=True))
    prob_grad = jnp.einsum('qhd,kd->hqk', grad_grp, value_head)
    row_dot = lax.optimization_barrier(jnp.sum(attn_probs * prob_grad, axis=-1, keepdims=True))
    score_grad = (attn_probs * (prob_grad - row_dot)).astype(jnp.bfloat16)
    probs_low = attn_probs.astype(jnp.bfloat16)
    score_grad, probs_low = lax.optimization_barrier((score_grad, probs_low))
    score_wide = score_grad.astype(jnp.float32)
    probs_wide = probs_low.astype(jnp.float32)
    query_gradient = (jnp.einsum('hqk,kd->qhd', score_wide, key_head) * inv_root).astype(jnp.bfloat16)
    key_gradient_rows = (jnp.einsum('hqk,qhd->kd', score_wide, query_grp) * inv_root).astype(jnp.bfloat16)
    value_gradient_rows = jnp.einsum('hqk,qhd->kd', probs_wide, grad_grp).astype(jnp.bfloat16)
    return (query_gradient, key_gradient_rows, value_gradient_rows)

def rollout_gradient_list(inputs):
    rollout_queries, rollout_keys, rollout_values, rollout_gradients, doc_ids = inputs
    heads_of_queries = rollout_queries.astype(jnp.float32).reshape(ROLLOUT_LENGTH, KEY_VALUE_HEADS, GROUP_QUERIES, HEAD_SIZE).transpose(1, 0, 2, 3)
    head_gradient = rollout_gradients.astype(jnp.float32).reshape(ROLLOUT_LENGTH, KEY_VALUE_HEADS, GROUP_QUERIES, HEAD_SIZE).transpose(1, 0, 2, 3)
    heads_of_keys = rollout_keys.astype(jnp.float32).reshape(ROLLOUT_LENGTH, KEY_VALUE_HEADS, HEAD_SIZE).transpose(1, 0, 2)
    heads_of_values = rollout_values.astype(jnp.float32).reshape(ROLLOUT_LENGTH, KEY_VALUE_HEADS, HEAD_SIZE).transpose(1, 0, 2)

    def one_group(group_in):
        return group_grads(group_in[0], group_in[1], group_in[2], group_in[3], doc_ids)
    query_gradient, key_gradient_rows, value_gradient_rows = lax.map(one_group, (heads_of_queries, heads_of_keys, heads_of_values, head_gradient))
    return (query_gradient.transpose(1, 0, 2, 3).reshape(ROLLOUT_LENGTH, QUERY_HEADS * HEAD_SIZE), key_gradient_rows.transpose(1, 0, 2).reshape(ROLLOUT_LENGTH, KEY_VALUE_HEADS * HEAD_SIZE), value_gradient_rows.transpose(1, 0, 2).reshape(ROLLOUT_LENGTH, KEY_VALUE_HEADS * HEAD_SIZE))

def reference(hidden_in, queries, keys, values, output_gradient, document_index):
    query_gradient, key_gradient_rows, value_gradient_rows = lax.map(rollout_gradient_list, (queries.reshape(ROLLOUT_COUNT, ROLLOUT_LENGTH, QUERY_HEADS * HEAD_SIZE), keys.reshape(ROLLOUT_COUNT, ROLLOUT_LENGTH, KEY_VALUE_HEADS * HEAD_SIZE), values.reshape(ROLLOUT_COUNT, ROLLOUT_LENGTH, KEY_VALUE_HEADS * HEAD_SIZE), output_gradient.reshape(ROLLOUT_COUNT, ROLLOUT_LENGTH, QUERY_HEADS * HEAD_SIZE), document_index))
    grad_queries = query_gradient.reshape(TOKEN_COUNT, QUERY_HEADS * HEAD_SIZE)
    key_gradient = key_gradient_rows.reshape(TOKEN_COUNT, KEY_VALUE_HEADS * HEAD_SIZE)
    value_gradient = value_gradient_rows.reshape(TOKEN_COUNT, KEY_VALUE_HEADS * HEAD_SIZE)
    weight_sum = lax.dot_general(hidden_in, value_gradient, (((0,), (0,)), ((), ())), preferred_element_type=jnp.float32)
    value_weight_grad = weight_sum * (1.0 / math.sqrt(TOKEN_COUNT))
    return (grad_queries, key_gradient, value_gradient, value_weight_grad)
```

```python
import functools
import math

import jax
import jax.numpy as jnp
from jax import lax
from jax.experimental import pallas as pl
from jax.experimental.pallas import tpu as pltpu
from jax.sharding import PartitionSpec as P

HEAD = 128
MESH = pl.DeviceIdType.MESH
F32 = jnp.float32
BF16 = jnp.bfloat16
NT = (((1,), (1,)), ((), ()))
TN = (((0,), (0,)), ((), ()))


def kernel(
    n_dp, n_ctx, inner,
    hid_hbm, q_hbm, k_hbm, v_hbm, o_hbm, doc_hbm,
    dq, dk_out, dv_out, dw,
    hid, q, o, doc, hid_t, slab, kv, docwin, bias, dk_acc, dv_acc, part, part_in, dv_all,
    y_out, y_in, z_out, z_in,
    load_sem, key_sem, doc_send, doc_recv, kv_send, kv_recv, hid_send, hid_recv, part_send, part_recv,
    dv_send, fw_send, dv_recv, y_send, y_recv, z_send, z_recv,
):
    tokens = q.shape[0]
    width = hid.shape[1]
    outer = n_dp // inner
    chips = n_ctx // 2
    members = inner * 2
    rows = width // (n_dp * n_ctx)
    window = n_ctx // 2 + 1
    last = window - 1
    kv_heads = kv.shape[0]
    group = q.shape[1] // (kv_heads * HEAD)
    inv_root = 1.0 / math.sqrt(HEAD)
    dp = lax.axis_index("dp")
    c = lax.axis_index("ctx")
    far = dp // inner
    near = lax.rem(dp, inner)
    core = lax.rem(c, 2)
    chip = c // 2
    mine = near * 2 + core
    sibling = (dp, c + 1 - 2 * core)

    def member(j):
        return (far * inner + j // 2, chip * 2 + lax.rem(j, 2))

    def across(step):
        return (lax.rem(far + step, outer) * inner + near, c)

    def beside(step):
        return (dp, lax.rem(chip + step, chips) * 2 + core)

    loads = [
        pltpu.make_async_copy(a, b, load_sem.at[n])
        for n, (a, b) in enumerate(((hid_hbm, hid), (q_hbm, q), (o_hbm, o), (doc_hbm, doc)))
    ]
    key_loads = [
        pltpu.make_async_copy(
            ref.at[:, g * HEAD:(g + 1) * HEAD], kv.at[g, last, n], key_sem.at[g, n]
        )
        for g in range(kv_heads) for n, ref in enumerate((k_hbm, v_hbm))
    ]
    loads[3].start()
    for copy in key_loads:
        copy.start()
    for copy in loads[:3]:
        copy.start()

    barrier = pltpu.get_barrier_semaphore()

    def greet(device):
        pl.semaphore_signal(barrier, inc=1, device_id=device, device_id_type=MESH)

    for step in range(1, n_ctx):
        greet((dp, lax.rem(c + step, n_ctx)))
    for step in range(1, members):
        greet(member(lax.rem(mine + step, members)))
    for step in range(1, outer):
        greet(across(step))
    loads[3].wait()
    docwin[last] = jnp.broadcast_to(doc[...], (8, tokens))
    for copy in key_loads:
        copy.wait()
    pl.semaphore_wait(barrier, n_ctx - 1 + members - 1 + outer - 1)

    def doc_copy(step, to):
        return pltpu.make_async_remote_copy(
            src_ref=docwin.at[last], dst_ref=docwin.at[last - step],
            send_sem=doc_send.at[step], recv_sem=doc_recv.at[step],
            device_id=(dp, to), device_id_type=MESH,
        )

    def kv_copy(g, step, to):
        return pltpu.make_async_remote_copy(
            src_ref=kv.at[g, last], dst_ref=kv.at[g, last - step],
            send_sem=kv_send.at[g, step], recv_sem=kv_recv.at[g, step],
            device_id=(dp, to), device_id_type=MESH,
        )

    for step in range(1, window):
        @pl.when(c + step < n_ctx)
        def _():
            doc_copy(step, c + step).start()

    def kv_start(g, carry):
        for step in range(1, window):
            @pl.when(c + step < n_ctx)
            def _():
                kv_copy(g, step, c + step).start()
        return carry

    lax.fori_loop(0, kv_heads, kv_start, 0)

    chunk = 512
    loads[0].wait()

    def turn(n, carry):
        at = pl.multiple_of(n * chunk, chunk)
        hid_t[pl.ds(at, chunk), :] = hid[:, pl.ds(at, chunk)].T
        return carry

    lax.fori_loop(0, width // chunk, turn, 0)

    def rows_of(j, y, z):
        at = ((z * inner + j // 2) * n_ctx + y * 2 + lax.rem(j, 2)) * rows
        return pl.ds(pl.multiple_of(at, rows), rows)

    my_lanes = pl.ds(pl.multiple_of(mine * tokens, tokens), tokens)

    def slab_rows(n):
        return slice(n * rows, (n + 1) * rows)

    def owner_rows(j, n):
        return rows_of(j, lax.rem(chip + n // outer, chips), lax.rem(far + n % outer, outer))

    def hid_copy(step, n):
        j = lax.rem(mine + step, members)
        return pltpu.make_async_remote_copy(
            src_ref=hid_t.at[owner_rows(j, n)],
            dst_ref=slab.at[slab_rows(n), my_lanes],
            send_sem=hid_send.at[n, step], recv_sem=hid_recv.at[n, mine],
            device_id=member(j), device_id_type=MESH,
        )

    blocks = chips * outer
    def hid_start(first, end):
        for n in range(end - 1, first - 1, -1):
            def one(step, carry):
                hid_copy(step, n).start()
                return carry

            lax.fori_loop(1, members, one, 0)

    hid_start(outer, blocks)
    for n in range(blocks):
        slab[slab_rows(n), my_lanes] = hid_t[owner_rows(mine, n)]

    for step in range(1, window):
        @pl.when(c >= step)
        def _():
            doc_copy(step, c).wait_recv()

        @pl.when(c < step)
        def _():
            docwin[last - step] = jnp.full((8, tokens), -1, jnp.int32)
            for g in range(kv_heads):
                kv[g, last - step] = jnp.zeros((2, tokens, HEAD), BF16)

    doc_query = jnp.broadcast_to(doc[...], (tokens, tokens))
    key_row = lax.broadcasted_iota(jnp.int32, (tokens, tokens), 0)
    query_col = lax.broadcasted_iota(jnp.int32, (tokens, tokens), 1)
    for b in range(window):
        doc_key = jnp.broadcast_to(docwin[b][0:1].astype(F32), (tokens, tokens)).T.astype(jnp.int32)
        allowed = doc_key == doc_query
        if b == last:
            allowed = allowed & (key_row <= query_col)
        else:
            allowed = allowed & (doc_key >= 0)
        tile = jnp.where(allowed, 0.0, -1e30)
        bias[b * tokens:(b + 1) * tokens] = jnp.concatenate([tile, tile], axis=1)

    span = window * tokens
    loads[1].wait()
    loads[2].wait()

    def part_copy(g, step, to):
        return pltpu.make_async_remote_copy(
            src_ref=part.at[g, last - step], dst_ref=part_in.at[g, step],
            send_sem=part_send.at[g, step], recv_sem=part_recv.at[g, step],
            device_id=(dp, to), device_id_type=MESH,
        )

    def source(step):
        return 2 * lax.rem(near + inner - step, inner) + core

    def block(j):
        return pl.ds(pl.multiple_of(j * tokens, tokens), tokens)

    def dv_copy(g, step):
        return pltpu.make_async_remote_copy(
            src_ref=dv_all.at[g, block(mine)], dst_ref=dv_all.at[g, block(mine)],
            send_sem=dv_send.at[g, step], recv_sem=dv_recv.at[g, mine],
            device_id=member(2 * lax.rem(near + step, inner) + core), device_id_type=MESH,
        )

    def fw_copy(g, step):
        j = source(step)
        return pltpu.make_async_remote_copy(
            src_ref=dv_all.at[g, block(j)], dst_ref=dv_all.at[g, block(j)],
            send_sem=fw_send.at[g, step], recv_sem=dv_recv.at[g, j],
            device_id=sibling, device_id_type=MESH,
        )

    def arrived(g, j):
        pltpu.make_async_remote_copy(
            src_ref=dv_all.at[g, block(j)], dst_ref=dv_all.at[g, block(j)],
            send_sem=dv_send.at[g, 0], recv_sem=dv_recv.at[g, j],
            device_id=sibling, device_id_type=MESH,
        ).wait_recv()

    def finish(g):
        for step in range(1, window):
            @pl.when(c + step < n_ctx)
            def _():
                part_copy(g, step, c).wait_recv()

            @pl.when(c + step >= n_ctx)
            def _():
                part_in[g, step] = jnp.zeros((2, tokens, HEAD), part_in.dtype)

        cols = pl.ds(pl.multiple_of(g * HEAD, HEAD), HEAD)
        sums = []
        for n in range(2):
            total = part[g, last, n].astype(F32)
            for step in range(1, window):
                total = total + part_in[g, step, n].astype(F32)
            sums.append(total.astype(BF16))
        dk_out[:, cols] = sums[0]
        dv_out[:, cols] = sums[1]
        dv_all[g, block(mine)] = sums[1]
        for step in range(1, inner):
            dv_copy(g, step).start()
        fw_copy(g, 0).start()

    def hid_wait(first, end):
        def one(step, carry):
            j = lax.rem(mine + members - step, members)
            for n in range(first, end):
                pltpu.make_async_remote_copy(
                    src_ref=hid_t.at[pl.ds(0, rows)], dst_ref=slab.at[slab_rows(n), block(j)],
                    send_sem=hid_send.at[n, step], recv_sem=hid_recv.at[n, j],
                    device_id=sibling, device_id_type=MESH,
                ).wait_recv()
            return carry

        lax.fori_loop(1, members, one, 0)

    scale = 1.0 / math.sqrt(tokens * n_dp * n_ctx)

    def product(g, first, end):
        left = slab[first * rows:end * rows, :]
        return jnp.dot(left, dv_all[g], preferred_element_type=F32) * scale

    def y_copy(g, step):
        return pltpu.make_async_remote_copy(
            src_ref=y_out.at[g, step], dst_ref=y_in.at[g, step],
            send_sem=y_send.at[g, step], recv_sem=y_recv.at[g, step],
            device_id=beside(step), device_id_type=MESH,
        )

    def z_copy(g, step):
        return pltpu.make_async_remote_copy(
            src_ref=z_out.at[g, step], dst_ref=z_in.at[g, step],
            send_sem=z_send.at[g, step], recv_sem=z_recv.at[g, step],
            device_id=across(step), device_id_type=MESH,
        )

    def multiply(g, carry):
        for step in range(1, inner):
            arrived(g, source(step))
            fw_copy(g, step).start()
        for step in range(inner):
            arrived(g, source(step) + 1 - 2 * core)
        for step in range(1, chips):
            y_out[g, step] = product(g, step * outer, (step + 1) * outer).astype(BF16)
            y_copy(g, step).start()
        return carry

    def join(g, carry):
        for step in range(1, chips):
            y_copy(g, step).wait_recv()
        for step in range(1, outer):
            total = product(g, step, step + 1)
            for y in range(1, chips):
                total = total + y_in[g, y, slab_rows(step)].astype(F32)
            z_out[g, step] = total.astype(BF16)
            z_copy(g, step).start()
        return carry

    def close(g):
        total = product(g, 0, 1)
        for y in range(1, chips):
            total = total + y_in[g, y, slab_rows(0)].astype(F32)
        for step in range(1, outer):
            z_copy(g, step).wait_recv()
            total = total + z_in[g, step].astype(F32)
        dw[:, pl.ds(pl.multiple_of(g * HEAD, HEAD), HEAD)] = total

    def one_head(g, carry):
        for step in range(1, window):
            @pl.when(c >= step)
            def _():
                kv_copy(g, step, c).wait_recv()

        key_rows = kv[g, :, 0].reshape(span, HEAD)
        value_rows = kv[g, :, 1].reshape(span, HEAD)
        for h in range(0, group, 2):
            at = [pl.ds(pl.multiple_of((g * group + h + n) * HEAD, HEAD), HEAD) for n in range(2)]
            q2 = jnp.concatenate([q[:, at[0]], q[:, at[1]]], axis=0)
            o2 = jnp.concatenate([o[:, at[0]], o[:, at[1]]], axis=0)
            s = lax.dot_general(key_rows, q2, NT, preferred_element_type=F32)
            s = s * inv_root + bias[...]
            e = jnp.exp(s - jnp.max(s, axis=0, keepdims=True))
            p = e * (1.0 / jnp.sum(e, axis=0, keepdims=True))
            t = lax.dot_general(value_rows, o2, NT, preferred_element_type=F32)
            row_dot = jnp.sum(p * t, axis=0, keepdims=True)
            ds = (p * (t - row_dot)).astype(BF16)
            low = p.astype(BF16)
            dk = jnp.dot(ds, q2, preferred_element_type=F32)
            dv = jnp.dot(low, o2, preferred_element_type=F32)
            if h == 0:
                dk_acc[...] = dk
                dv_acc[...] = dv
            else:
                dk_acc[...] += dk
                dv_acc[...] += dv
            dq_t = lax.dot_general(key_rows, ds, TN, preferred_element_type=F32) * inv_root
            for n in range(2):
                dq[:, at[n]] = dq_t[:, n * tokens:(n + 1) * tokens].T.astype(BF16)
        for b in range(window):
            blk = slice(b * tokens, (b + 1) * tokens)
            part[g, b, 0] = (dk_acc[blk] * inv_root).astype(part.dtype)
            part[g, b, 1] = dv_acc[blk].astype(part.dtype)
        for step in range(1, window):
            @pl.when(c >= step)
            def _():
                part_copy(g, step, c - step).start()

        @pl.when(g >= 1)
        def _():
            finish(g - 1)

        return carry

    lax.fori_loop(0, kv_heads, one_head, 0)
    finish(kv_heads - 1)
    hid_start(0, outer)

    hid_wait(outer, blocks)
    lax.fori_loop(0, kv_heads, multiply, 0)
    hid_wait(1, outer)
    lax.fori_loop(0, kv_heads, join, 0)
    hid_wait(0, 1)

    def sent(g, carry):
        close(g)
        for step in range(1, window):
            @pl.when(c + step < n_ctx)
            def _():
                kv_copy(g, step, c + step).wait_send()

            @pl.when(c >= step)
            def _():
                part_copy(g, step, c - step).wait_send()

        for step in range(1, inner):
            dv_copy(g, step).wait_send()
            fw_copy(g, step).wait_send()
        fw_copy(g, 0).wait_send()
        for step in range(1, chips):
            y_copy(g, step).wait_send()
        for step in range(1, outer):
            z_copy(g, step).wait_send()
        return carry

    lax.fori_loop(0, kv_heads, sent, 0)
    for step in range(1, window):
        @pl.when(c + step < n_ctx)
        def _():
            doc_copy(step, c + step).wait_send()

    def hid_sent(step, carry):
        for n in range(blocks):
            hid_copy(step, n).wait_send()
        return carry

    lax.fori_loop(1, members, hid_sent, 0)


def shards(hidden_in, queries, keys, values, output_gradient, document_index):
    n_dp = lax.axis_size("dp")
    n_ctx = lax.axis_size("ctx")
    tokens, width = hidden_in.shape
    kv_width = keys.shape[1]
    heads = kv_width // HEAD
    inner = min(4, n_dp)
    outer = n_dp // inner
    chips = n_ctx // 2
    members = inner * 2
    rows = width // (n_dp * n_ctx)
    window = n_ctx // 2 + 1
    span = window * tokens
    dma = pltpu.SemaphoreType.DMA
    vmem = pl.BlockSpec(memory_space=pltpu.VMEM)
    hbm = pl.BlockSpec(memory_space=pltpu.HBM)
    return write_out(*pl.pallas_call(
        functools.partial(kernel, n_dp, n_ctx, inner),
        out_shape=(
            pltpu.VMEM(queries.shape, BF16),
            pltpu.VMEM(keys.shape, BF16),
            pltpu.VMEM(values.shape, BF16),
            pltpu.VMEM((rows, kv_width), F32),
        ),
        in_specs=[hbm] * 6,
        out_specs=(vmem,) * 4,
        scratch_shapes=[
            pltpu.VMEM(hidden_in.shape, BF16),
            pltpu.VMEM(queries.shape, BF16),
            pltpu.VMEM(queries.shape, BF16),
            pltpu.VMEM(document_index.shape, jnp.int32),
            pltpu.VMEM((width, tokens), BF16),
            pltpu.VMEM((chips * outer * rows, members * tokens), BF16),
            pltpu.VMEM((heads, window, 2, tokens, HEAD), BF16),
            pltpu.VMEM((window, 8, tokens), jnp.int32),
            pltpu.VMEM((span, 2 * tokens), F32),
            pltpu.VMEM((span, HEAD), F32),
            pltpu.VMEM((span, HEAD), F32),
            pltpu.VMEM((heads, window, 2, tokens, HEAD), BF16),
            pltpu.VMEM((heads, window, 2, tokens, HEAD), BF16),
            pltpu.VMEM((heads, members * tokens, HEAD), BF16),
            pltpu.VMEM((heads, chips, outer * rows, HEAD), BF16),
            pltpu.VMEM((heads, chips, outer * rows, HEAD), BF16),
            pltpu.VMEM((heads, outer, rows, HEAD), BF16),
            pltpu.VMEM((heads, outer, rows, HEAD), BF16),
            dma((4,)), dma((heads, 2)), dma((window,)), dma((window,)),
            dma((heads, window)), dma((heads, window)),
            dma((chips * outer, members)), dma((chips * outer, members)),
            dma((heads, window)), dma((heads, window)),
            dma((heads, inner)), dma((heads, inner)), dma((heads, members)),
            dma((heads, chips)), dma((heads, chips)),
            dma((heads, outer)), dma((heads, outer)),
        ],
        compiler_params=pltpu.CompilerParams(
            collective_id=0, has_side_effects=True, vmem_limit_bytes=58 * 1024 * 1024
        ),
    )(hidden_in, queries, keys, values, output_gradient, document_index))


def store(*refs):
    n = (len(refs) - 1) // 2
    sem = refs[-1]
    copies = [
        pltpu.make_async_copy(a, b, sem.at[i])
        for i, (a, b) in enumerate(zip(refs[:n], refs[n:2 * n]))
    ]
    for copy in copies:
        copy.start()
    for copy in copies:
        copy.wait()


def write_out(*arrays):
    return pl.pallas_call(
        store,
        out_shape=tuple(jax.ShapeDtypeStruct(a.shape, a.dtype) for a in arrays),
        in_specs=[pl.BlockSpec(memory_space=pltpu.VMEM)] * len(arrays),
        out_specs=(pl.BlockSpec(memory_space=pltpu.HBM),) * len(arrays),
        scratch_shapes=[pltpu.SemaphoreType.DMA((len(arrays),))],
        compiler_params=pltpu.CompilerParams(vmem_limit_bytes=8 * 1024 * 1024),
    )(*arrays)


def solution(mesh):
    return jax.shard_map(
        shards,
        mesh=mesh,
        in_specs=(P(("dp", "ctx"), None),) * 5 + (P("dp", "ctx"),),
        out_specs=(P(("dp", "ctx"), None),) * 4,
        check_vma=False,
    )
```

```python
import functools
import math

import jax
import jax.numpy as jnp
from jax import lax
from jax.experimental import pallas as pl
from jax.experimental.pallas import tpu as pltpu
from jax.sharding import PartitionSpec as P

HEAD = 128
MESH = pl.DeviceIdType.MESH
F32 = jnp.float32
BF16 = jnp.bfloat16
NT = (((1,), (1,)), ((), ()))
TN = (((0,), (0,)), ((), ()))


def kernel(
    n_dp, n_ctx, inner,
    hid_hbm, q_hbm, k_hbm, v_hbm, o_hbm, doc_hbm,
    dq, dk_out, dv_out, dw,
    hid, q, o, doc, hid_t, slab, kv, docwin, bias, dk_acc, dv_acc, part, part_in, dv_all,
    y_out, y_in, z_out, z_in,
    load_sem, key_sem, doc_send, doc_recv, kv_send, kv_recv, hid_send, hid_recv, part_send, part_recv,
    dv_send, fw_send, dv_recv, y_send, y_recv, z_send, z_recv,
):
    tokens = q.shape[0]
    width = hid.shape[1]
    outer = n_dp // inner
    chips = n_ctx // 2
    members = inner * 2
    rows = width // (n_dp * n_ctx)
    window = n_ctx // 2 + 1
    last = window - 1
    kv_heads = kv.shape[0]
    group = q.shape[1] // (kv_heads * HEAD)
    inv_root = 1.0 / math.sqrt(HEAD)
    dp = lax.axis_index("dp")
    c = lax.axis_index("ctx")
    far = dp // inner
    near = lax.rem(dp, inner)
    core = lax.rem(c, 2)
    chip = c // 2
    mine = near * 2 + core
    sibling = (dp, c + 1 - 2 * core)

    def member(j):
        return (far * inner + j // 2, chip * 2 + lax.rem(j, 2))

    def across(step):
        return (lax.rem(far + step, outer) * inner + near, c)

    def beside(step):
        return (dp, lax.rem(chip + step, chips) * 2 + core)

    loads = [
        pltpu.make_async_copy(a, b, load_sem.at[n])
        for n, (a, b) in enumerate(((hid_hbm, hid), (q_hbm, q), (o_hbm, o), (doc_hbm, doc)))
    ]
    key_loads = [
        pltpu.make_async_copy(
            ref.at[:, g * HEAD:(g + 1) * HEAD], kv.at[g, last, n], key_sem.at[g, n]
        )
        for g in range(kv_heads) for n, ref in enumerate((k_hbm, v_hbm))
    ]
    loads[3].start()
    for copy in key_loads:
        copy.start()
    for copy in loads[:3]:
        copy.start()

    barrier = pltpu.get_barrier_semaphore()

    def greet(device):
        pl.semaphore_signal(barrier, inc=1, device_id=device, device_id_type=MESH)

    for step in range(1, n_ctx):
        greet((dp, lax.rem(c + step, n_ctx)))
    for step in range(1, members):
        greet(member(lax.rem(mine + step, members)))
    for step in range(1, outer):
        greet(across(step))
    loads[3].wait()
    docwin[last] = jnp.broadcast_to(doc[...], (8, tokens))
    for copy in key_loads:
        copy.wait()
    pl.semaphore_wait(barrier, n_ctx - 1 + members - 1 + outer - 1)

    def doc_copy(step, to):
        return pltpu.make_async_remote_copy(
            src_ref=docwin.at[last], dst_ref=docwin.at[last - step],
            send_sem=doc_send.at[step], recv_sem=doc_recv.at[step],
            device_id=(dp, to), device_id_type=MESH,
        )

    def kv_copy(g, step, to):
        return pltpu.make_async_remote_copy(
            src_ref=kv.at[g, last], dst_ref=kv.at[g, last - step],
            send_sem=kv_send.at[g, step], recv_sem=kv_recv.at[g, step],
            device_id=(dp, to), device_id_type=MESH,
        )

    for step in range(1, window):
        @pl.when(c + step < n_ctx)
        def _():
            doc_copy(step, c + step).start()

    def kv_start(g, carry):
        for step in range(1, window):
            @pl.when(c + step < n_ctx)
            def _():
                kv_copy(g, step, c + step).start()
        return carry

    lax.fori_loop(0, kv_heads, kv_start, 0)

    chunk = 512
    loads[0].wait()

    def turn(n, carry):
        at = pl.multiple_of(n * chunk, chunk)
        hid_t[pl.ds(at, chunk), :] = hid[:, pl.ds(at, chunk)].T
        return carry

    lax.fori_loop(0, width // chunk, turn, 0)

    def rows_of(j, y, z):
        at = ((z * inner + j // 2) * n_ctx + y * 2 + lax.rem(j, 2)) * rows
        return pl.ds(pl.multiple_of(at, rows), rows)

    my_lanes = pl.ds(pl.multiple_of(mine * tokens, tokens), tokens)

    def slab_rows(n):
        return slice(n * rows, (n + 1) * rows)

    def owner_rows(j, n):
        return rows_of(j, lax.rem(chip + n // outer, chips), lax.rem(far + n % outer, outer))

    def hid_copy(step, n):
        j = lax.rem(mine + step, members)
        return pltpu.make_async_remote_copy(
            src_ref=hid_t.at[owner_rows(j, n)],
            dst_ref=slab.at[slab_rows(n), my_lanes],
            send_sem=hid_send.at[n, step], recv_sem=hid_recv.at[n, mine],
            device_id=member(j), device_id_type=MESH,
        )

    blocks = chips * outer
    def hid_start(first, end):
        for n in range(end - 1, first - 1, -1):
            def one(step, carry):
                hid_copy(step, n).start()
                return carry

            lax.fori_loop(1, members, one, 0)

    hid_start(outer, blocks)
    for n in range(blocks):
        slab[slab_rows(n), my_lanes] = hid_t[owner_rows(mine, n)]

    for step in range(1, window):
        @pl.when(c >= step)
        def _():
            doc_copy(step, c).wait_recv()

        @pl.when(c < step)
        def _():
            docwin[last - step] = jnp.full((8, tokens), -1, jnp.int32)
            for g in range(kv_heads):
                kv[g, last - step] = jnp.zeros((2, tokens, HEAD), BF16)

    doc_query = jnp.broadcast_to(doc[...], (tokens, tokens))
    key_row = lax.broadcasted_iota(jnp.int32, (tokens, tokens), 0)
    query_col = lax.broadcasted_iota(jnp.int32, (tokens, tokens), 1)
    for b in range(window):
        doc_key = jnp.broadcast_to(docwin[b][0:1].astype(F32), (tokens, tokens)).T.astype(jnp.int32)
        allowed = doc_key == doc_query
        if b == last:
            allowed = allowed & (key_row <= query_col)
        else:
            allowed = allowed & (doc_key >= 0)
        tile = jnp.where(allowed, 0.0, -1e30)
        bias[b * tokens:(b + 1) * tokens] = jnp.concatenate([tile, tile], axis=1)

    span = window * tokens
    loads[1].wait()
    loads[2].wait()

    def part_copy(g, step, to):
        return pltpu.make_async_remote_copy(
            src_ref=part.at[g, last - step], dst_ref=part_in.at[g, step],
            send_sem=part_send.at[g, step], recv_sem=part_recv.at[g, step],
            device_id=(dp, to), device_id_type=MESH,
        )

    def source(step):
        return 2 * lax.rem(near + inner - step, inner) + core

    def block(j):
        return pl.ds(pl.multiple_of(j * tokens, tokens), tokens)

    def dv_copy(g, step):
        return pltpu.make_async_remote_copy(
            src_ref=dv_all.at[g, block(mine)], dst_ref=dv_all.at[g, block(mine)],
            send_sem=dv_send.at[g, step], recv_sem=dv_recv.at[g, mine],
            device_id=member(2 * lax.rem(near + step, inner) + core), device_id_type=MESH,
        )

    def fw_copy(g, step):
        j = source(step)
        return pltpu.make_async_remote_copy(
            src_ref=dv_all.at[g, block(j)], dst_ref=dv_all.at[g, block(j)],
            send_sem=fw_send.at[g, step], recv_sem=dv_recv.at[g, j],
            device_id=sibling, device_id_type=MESH,
        )

    def arrived(g, j):
        pltpu.make_async_remote_copy(
            src_ref=dv_all.at[g, block(j)], dst_ref=dv_all.at[g, block(j)],
            send_sem=dv_send.at[g, 0], recv_sem=dv_recv.at[g, j],
            device_id=sibling, device_id_type=MESH,
        ).wait_recv()

    def finish(g):
        for step in range(1, window):
            @pl.when(c + step < n_ctx)
            def _():
                part_copy(g, step, c).wait_recv()

            @pl.when(c + step >= n_ctx)
            def _():
                part_in[g, step] = jnp.zeros((2, tokens, HEAD), part_in.dtype)

        cols = pl.ds(pl.multiple_of(g * HEAD, HEAD), HEAD)
        sums = []
        for n in range(2):
            total = part[g, last, n].astype(F32)
            for step in range(1, window):
                total = total + part_in[g, step, n].astype(F32)
            sums.append(total.astype(BF16))
        dk_out[:, cols] = sums[0]
        dv_out[:, cols] = sums[1]
        dv_all[g, block(mine)] = sums[1]
        for step in range(1, inner):
            dv_copy(g, step).start()
        fw_copy(g, 0).start()

    def hid_wait(first, end):
        def one(step, carry):
            j = lax.rem(mine + members - step, members)
            for n in range(first, end):
                pltpu.make_async_remote_copy(
                    src_ref=hid_t.at[pl.ds(0, rows)], dst_ref=slab.at[slab_rows(n), block(j)],
                    send_sem=hid_send.at[n, step], recv_sem=hid_recv.at[n, j],
                    device_id=sibling, device_id_type=MESH,
                ).wait_recv()
            return carry

        lax.fori_loop(1, members, one, 0)

    scale = 1.0 / math.sqrt(tokens * n_dp * n_ctx)

    def product(g, first, end):
        left = slab[first * rows:end * rows, :]
        return jnp.dot(left, dv_all[g], preferred_element_type=F32) * scale

    def y_copy(g, step):
        return pltpu.make_async_remote_copy(
            src_ref=y_out.at[g, step], dst_ref=y_in.at[g, step],
            send_sem=y_send.at[g, step], recv_sem=y_recv.at[g, step],
            device_id=beside(step), device_id_type=MESH,
        )

    def z_copy(g, step):
        return pltpu.make_async_remote_copy(
            src_ref=z_out.at[g, step], dst_ref=z_in.at[g, step],
            send_sem=z_send.at[g, step], recv_sem=z_recv.at[g, step],
            device_id=across(step), device_id_type=MESH,
        )

    def multiply(g, carry):
        for step in range(1, inner):
            arrived(g, source(step))
            fw_copy(g, step).start()
        for step in range(inner):
            arrived(g, source(step) + 1 - 2 * core)
        for step in range(1, chips):
            y_out[g, step] = product(g, step * outer, (step + 1) * outer).astype(BF16)
            y_copy(g, step).start()
        return carry

    def join(g, carry):
        for step in range(1, chips):
            y_copy(g, step).wait_recv()
        for step in range(1, outer):
            total = product(g, step, step + 1)
            for y in range(1, chips):
                total = total + y_in[g, y, slab_rows(step)].astype(F32)
            z_out[g, step] = total.astype(BF16)
            z_copy(g, step).start()
        return carry

    def close(g):
        total = product(g, 0, 1)
        for y in range(1, chips):
            total = total + y_in[g, y, slab_rows(0)].astype(F32)
        for step in range(1, outer):
            z_copy(g, step).wait_recv()
            total = total + z_in[g, step].astype(F32)
        dw[:, pl.ds(pl.multiple_of(g * HEAD, HEAD), HEAD)] = total

    def one_head(g, carry):
        for step in range(1, window):
            @pl.when(c >= step)
            def _():
                kv_copy(g, step, c).wait_recv()

        key_rows = kv[g, :, 0].reshape(span, HEAD)
        value_rows = kv[g, :, 1].reshape(span, HEAD)
        for h in range(0, group, 2):
            at = [pl.ds(pl.multiple_of((g * group + h + n) * HEAD, HEAD), HEAD) for n in range(2)]
            q2 = jnp.concatenate([q[:, at[0]], q[:, at[1]]], axis=0)
            o2 = jnp.concatenate([o[:, at[0]], o[:, at[1]]], axis=0)
            s = lax.dot_general(key_rows, q2, NT, preferred_element_type=F32)
            s = s * inv_root + bias[...]
            e = jnp.exp(s - jnp.max(s, axis=0, keepdims=True))
            p = e * (1.0 / jnp.sum(e, axis=0, keepdims=True))
            t = lax.dot_general(value_rows, o2, NT, preferred_element_type=F32)
            row_dot = jnp.sum(p * t, axis=0, keepdims=True)
            ds = (p * (t - row_dot)).astype(BF16)
            low = p.astype(BF16)
            dk = jnp.dot(ds, q2, preferred_element_type=F32)
            dv = jnp.dot(low, o2, preferred_element_type=F32)
            if h == 0:
                dk_acc[...] = dk
                dv_acc[...] = dv
            else:
                dk_acc[...] += dk
                dv_acc[...] += dv
            dq_t = lax.dot_general(key_rows, ds, TN, preferred_element_type=F32) * inv_root
            for n in range(2):
                dq[:, at[n]] = dq_t[:, n * tokens:(n + 1) * tokens].T.astype(BF16)
        for b in range(window):
            blk = slice(b * tokens, (b + 1) * tokens)
            part[g, b, 0] = (dk_acc[blk] * inv_root).astype(part.dtype)
            part[g, b, 1] = dv_acc[blk].astype(part.dtype)
        for step in range(1, window):
            @pl.when(c >= step)
            def _():
                part_copy(g, step, c - step).start()

        @pl.when(g >= 1)
        def _():
            finish(g - 1)

        return carry

    lax.fori_loop(0, kv_heads, one_head, 0)
    finish(kv_heads - 1)
    hid_start(0, outer)

    hid_wait(outer, blocks)
    lax.fori_loop(0, kv_heads, multiply, 0)
    hid_wait(1, outer)
    lax.fori_loop(0, kv_heads, join, 0)
    hid_wait(0, 1)

    def sent(g, carry):
        close(g)
        for step in range(1, window):
            @pl.when(c + step < n_ctx)
            def _():
                kv_copy(g, step, c + step).wait_send()

            @pl.when(c >= step)
            def _():
                part_copy(g, step, c - step).wait_send()

        for step in range(1, inner):
            dv_copy(g, step).wait_send()
            fw_copy(g, step).wait_send()
        fw_copy(g, 0).wait_send()
        for step in range(1, chips):
            y_copy(g, step).wait_send()
        for step in range(1, outer):
            z_copy(g, step).wait_send()
        return carry

    lax.fori_loop(0, kv_heads, sent, 0)
    for step in range(1, window):
        @pl.when(c + step < n_ctx)
        def _():
            doc_copy(step, c + step).wait_send()

    def hid_sent(step, carry):
        for n in range(blocks):
            hid_copy(step, n).wait_send()
        return carry

    lax.fori_loop(1, members, hid_sent, 0)


def general_call(hidden_in, queries, keys, values, output_gradient, document_index):
    n_dp = lax.axis_size("dp")
    n_ctx = lax.axis_size("ctx")
    tokens, width = hidden_in.shape
    kv_width = keys.shape[1]
    heads = kv_width // HEAD
    inner = min(4, n_dp)
    outer = n_dp // inner
    chips = n_ctx // 2
    members = inner * 2
    rows = width // (n_dp * n_ctx)
    window = n_ctx // 2 + 1
    span = window * tokens
    dma = pltpu.SemaphoreType.DMA
    vmem = pl.BlockSpec(memory_space=pltpu.VMEM)
    hbm = pl.BlockSpec(memory_space=pltpu.HBM)
    return pl.pallas_call(
        functools.partial(kernel, n_dp, n_ctx, inner),
        out_shape=(
            pltpu.VMEM(queries.shape, BF16),
            pltpu.VMEM(keys.shape, BF16),
            pltpu.VMEM(values.shape, BF16),
            pltpu.VMEM((rows, kv_width), F32),
        ),
        in_specs=[hbm] * 6,
        out_specs=(vmem,) * 4,
        scratch_shapes=[
            pltpu.VMEM(hidden_in.shape, BF16),
            pltpu.VMEM(queries.shape, BF16),
            pltpu.VMEM(queries.shape, BF16),
            pltpu.VMEM(document_index.shape, jnp.int32),
            pltpu.VMEM((width, tokens), BF16),
            pltpu.VMEM((chips * outer * rows, members * tokens), BF16),
            pltpu.VMEM((heads, window, 2, tokens, HEAD), BF16),
            pltpu.VMEM((window, 8, tokens), jnp.int32),
            pltpu.VMEM((span, 2 * tokens), F32),
            pltpu.VMEM((span, HEAD), F32),
            pltpu.VMEM((span, HEAD), F32),
            pltpu.VMEM((heads, window, 2, tokens, HEAD), BF16),
            pltpu.VMEM((heads, window, 2, tokens, HEAD), BF16),
            pltpu.VMEM((heads, members * tokens, HEAD), BF16),
            pltpu.VMEM((heads, chips, outer * rows, HEAD), BF16),
            pltpu.VMEM((heads, chips, outer * rows, HEAD), BF16),
            pltpu.VMEM((heads, outer, rows, HEAD), BF16),
            pltpu.VMEM((heads, outer, rows, HEAD), BF16),
            dma((4,)), dma((heads, 2)), dma((window,)), dma((window,)),
            dma((heads, window)), dma((heads, window)),
            dma((chips * outer, members)), dma((chips * outer, members)),
            dma((heads, window)), dma((heads, window)),
            dma((heads, inner)), dma((heads, inner)), dma((heads, members)),
            dma((heads, chips)), dma((heads, chips)),
            dma((heads, outer)), dma((heads, outer)),
        ],
        compiler_params=pltpu.CompilerParams(
            collective_id=0, has_side_effects=True, vmem_limit_bytes=58 * 1024 * 1024
        ),
    )(hidden_in, queries, keys, values, output_gradient, document_index)


DIM = {"x": 1, "l": 2, "h": 4, "y": 2, "k": 1}
PLANS = (("l", "x", "y", "h"),)
CHIPS = ("", "x", "l", "xl")
BLOCKS = ((1, 1), (1, 0), (0, 1), (0, 0))


def grouped(
    hid_hbm, q_hbm, k_hbm, v_hbm, o_hbm, doc_hbm,
    dq, dk_out, dv_out, dw,
    q, o, doc, slab, kv, docwin, bias, probs, dk_acc, dv_acc, part, part_in, dv_all,
    out1, in1, out2, in2, out3, in3,
    load_sem, key_sem, own_sem, doc_send, doc_recv, kv_send, kv_recv, hid_send, hid_recv,
    part_send, part_recv, dv_send, dv_recv, fw_send, fw_recv, send1, recv1, send2, recv2, send3, recv3,
):
    tokens = q.shape[0]
    width = slab.shape[-1]
    window = 3
    last = 2
    n_ctx = 4
    kv_heads = kv.shape[0]
    group = q.shape[1] // (kv_heads * HEAD)
    inv_root = 1.0 / math.sqrt(HEAD)
    scale = 1.0 / math.sqrt(tokens * 32)
    dp = lax.axis_index("dp")
    c = lax.axis_index("ctx")
    at = {"x": lax.rem(dp, 2), "l": lax.rem(dp // 2, 2), "h": dp // 4, "y": c // 2, "k": lax.rem(c, 2)}

    def place(flips):
        p = {d: 1 - at[d] if d in flips else at[d] for d in at}
        return (p["h"] * 4 + p["l"] * 2 + p["x"], p["y"] * 2 + p["k"])

    def remote(src, dst, send, recv, to):
        return pltpu.make_async_remote_copy(
            src_ref=src, dst_ref=dst, send_sem=send, recv_sem=recv,
            device_id=to, device_id_type=MESH,
        )

    loads = [
        pltpu.make_async_copy(a, b, load_sem.at[n])
        for n, (a, b) in enumerate(((q_hbm, q), (o_hbm, o), (doc_hbm, doc)))
    ]
    key_loads = [
        pltpu.make_async_copy(
            ref.at[:, g * HEAD:(g + 1) * HEAD], kv.at[g, last, n], key_sem.at[g, n]
        )
        for g in range(kv_heads) for n, ref in enumerate((k_hbm, v_hbm))
    ]
    loads[2].start()
    for copy in key_loads:
        copy.start()
    for copy in loads[:2]:
        copy.start()

    met = ("k", "y", "yk", "x", "xk", "l", "lk", "xl", "xlk", "xy", "xyk", "h")
    barrier = pltpu.get_barrier_semaphore()
    for flips in met:
        pl.semaphore_signal(barrier, inc=1, device_id=place(flips), device_id_type=MESH)

    def flips_of(dims, bits):
        return "".join(d for d, bit in zip(dims, bits) if bit)

    def hid_pair(p, n, m):
        e, x, r1, r2 = PLANS[p]
        member = flips_of((e, x, "k"), (m // 4, m // 2 % 2, m % 2))
        owner = member + flips_of((r1, r2), BLOCKS[n])
        row, col = place(owner)
        first = pl.multiple_of((row * n_ctx + col) * (len(PLANS) * width) + p * width, width)
        dst = slab.at[p, n, m * tokens:(m + 1) * tokens]
        return member, hid_hbm.at[:, pl.ds(first, width)], dst

    def hid_copy(p, n, m):
        member, src, dst = hid_pair(p, n, m)
        return remote(src, dst, hid_send.at[p, n, m], hid_recv.at[p, n, m], place(member))

    def hid_own(p, n):
        _, src, dst = hid_pair(p, n, 0)
        return pltpu.make_async_copy(src, dst, own_sem.at[p, n])

    def hid_start(p, n, members):
        for m in members:
            hid_copy(p, n, m).start()


    def hid_wait(p, n):
        hid_own(p, n).wait()
        for m in range(1, 8):
            hid_copy(p, n, m).wait_recv()

    loads[2].wait()
    docwin[last] = jnp.broadcast_to(doc[...], (8, tokens))
    for copy in key_loads:
        copy.wait()
    pl.semaphore_wait(barrier, len(met))

    def doc_copy(step, to):
        return remote(docwin.at[last], docwin.at[last - step], doc_send.at[step], doc_recv.at[step], (dp, to))

    def kv_copy(g, n, src, dst, to):
        return remote(kv.at[g, src, n], kv.at[g, dst, n], kv_send.at[g, n, dst], kv_recv.at[g, n, dst], place(to))

    def kv_far(g, n):
        return kv_copy(g, n, last, 0, "y")

    def kv_near(g, n):
        return kv_copy(g, n, last, 1, "k")

    def kv_pass(g, n):
        return kv_copy(g, n, 0, 1, "k")

    for step in range(1, window):
        @pl.when(c + step < n_ctx)
        def _():
            doc_copy(step, c + step).start()

    @pl.when(c < 2)
    def _():
        for n in range(2):
            lax.fori_loop(0, kv_heads, lambda g, carry: (kv_far(g, n).start(), carry)[1], 0)

    @pl.when(lax.rem(c, 2) == 0)
    def _():
        for n in range(2):
            lax.fori_loop(0, kv_heads, lambda g, carry: (kv_near(g, n).start(), carry)[1], 0)

    for n in (0, 2):
        hid_start(0, n, range(7, 0, -1))
        hid_own(0, n).start()

    for step in range(1, window):
        @pl.when(c >= step)
        def _():
            doc_copy(step, c).wait_recv()

        @pl.when(c < step)
        def _():
            docwin[last - step] = jnp.full((8, tokens), -1, jnp.int32)
            for g in range(kv_heads):
                kv[g, last - step] = jnp.zeros((2, tokens, HEAD), BF16)

    doc_query = jnp.broadcast_to(doc[...], (tokens, tokens))
    key_row = lax.broadcasted_iota(jnp.int32, (tokens, tokens), 0)
    query_col = lax.broadcasted_iota(jnp.int32, (tokens, tokens), 1)
    for b in range(window):
        doc_key = jnp.broadcast_to(docwin[b][0:1].astype(F32), (tokens, tokens)).T.astype(jnp.int32)
        allowed = doc_key == doc_query
        if b == last:
            allowed = allowed & (key_row <= query_col)
        else:
            allowed = allowed & (doc_key >= 0)
        tile = jnp.where(allowed, 0.0, -1e30)
        bias[b * tokens:(b + 1) * tokens] = jnp.concatenate([tile, tile], axis=1)

    span = window * tokens
    loads[0].wait()
    loads[1].wait()

    def part_copy(g, n, step, to):
        return remote(
            part.at[g, n, last - step], part_in.at[g, n, step],
            part_send.at[g, n, step], part_recv.at[g, n, step], (dp, to),
        )

    def part_start(g, n):
        for step in range(1, window):
            @pl.when(c >= step)
            def _():
                part_copy(g, n, step, c - step).start()

    def part_sum(g, n):
        for step in range(1, window):
            @pl.when(c + step < n_ctx)
            def _():
                part_copy(g, n, step, c).wait_recv()

            @pl.when(c + step >= n_ctx)
            def _():
                part_in[g, n, step] = jnp.zeros((tokens, HEAD), part_in.dtype)

        total = part[g, n, last].astype(F32)
        for step in range(1, window):
            total = total + part_in[g, n, step].astype(F32)
        return total

    def head_rows(g):
        if isinstance(g, int):
            return slice(g * HEAD, (g + 1) * HEAD)
        return pl.ds(pl.multiple_of(g * HEAD, HEAD), HEAD)

    def lanes(s, core):
        return slice((2 * s + core) * tokens, (2 * s + core + 1) * tokens)

    def dv_copy(g, s):
        rows = head_rows(g)
        return remote(
            dv_all.at[rows, lanes(0, 0)], dv_all.at[rows, lanes(s, 0)],
            dv_send.at[g, s], dv_recv.at[g, s], place(CHIPS[s]),
        )

    def fw_copy(g, s):
        rows = head_rows(g)
        return remote(
            dv_all.at[rows, lanes(s, 0)], dv_all.at[rows, lanes(s, 1)],
            fw_send.at[g, s], fw_recv.at[g, s], place("k"),
        )

    def finish(g):
        total = part_sum(g, 1)
        cols = head_rows(g)
        dv_out[:, cols] = total.astype(BF16)
        dv_all[cols, lanes(0, 0)] = total.T.astype(BF16)
        dv_copy(g, 1).start()
        for s in (3, 2):
            dv_copy(g, s).start()
        fw_copy(g, 0).start()

    def close(g):
        dk_out[:, head_rows(g)] = part_sum(g, 0).astype(BF16)

    def pass_on(g):
        dv_copy(g, 1).wait_recv()
        fw_copy(g, 1).start()
        for s in (2,):
            dv_copy(g, s).wait_recv()
            fw_copy(g, s).start()

    def pass_far(g):
        for s in (3,):
            dv_copy(g, s).wait_recv()
            fw_copy(g, s).start()

    def all_here(g):
        for s in range(4):
            fw_copy(g, s).wait_recv()

    def arrive(g, n):
        @pl.when(c >= 2)
        def _():
            kv_far(g, n).wait_recv()

        @pl.when(c == 3)
        def _():
            kv_pass(g, n).start()

        @pl.when(c >= 1)
        def _():
            kv_near(g, n).wait_recv()

    def two_heads(g, h):
        cols = [pl.ds(pl.multiple_of((g * group + h + n) * HEAD, HEAD), HEAD) for n in range(2)]
        q2 = jnp.concatenate([q[:, cols[0]], q[:, cols[1]]], axis=0)
        o2 = jnp.concatenate([o[:, cols[0]], o[:, cols[1]]], axis=0)
        return cols, q2, o2

    def attend(g):
        arrive(g, 0)
        key_rows = kv[g, :, 0].reshape(span, HEAD)
        for h in range(0, group, 2):
            _, q2, o2 = two_heads(g, h)
            s = lax.dot_general(key_rows, q2, NT, preferred_element_type=F32)
            s = s * inv_root + bias[...]
            e = jnp.exp(s - jnp.max(s, axis=0, keepdims=True))
            p = e * (1.0 / jnp.sum(e, axis=0, keepdims=True))
            probs[g, h // 2] = p
            dv = jnp.dot(p.astype(BF16), o2, preferred_element_type=F32)
            if h == 0:
                dv_acc[...] = dv
            else:
                dv_acc[...] += dv
        for b in range(window):
            part[g, 1, b] = dv_acc[b * tokens:(b + 1) * tokens].astype(part.dtype)
        part_start(g, 1)

    def descend(g, start, end):
        if start == 0:
            arrive(g, 1)
        key_rows = kv[g, :, 0].reshape(span, HEAD)
        value_rows = kv[g, :, 1].reshape(span, HEAD)
        for h in range(start, end, 2):
            cols, q2, o2 = two_heads(g, h)
            p = probs[g, h // 2]
            t = lax.dot_general(value_rows, o2, NT, preferred_element_type=F32)
            row_dot = jnp.sum(p * t, axis=0, keepdims=True)
            ds = (p * (t - row_dot)).astype(BF16)
            dk = jnp.dot(ds, q2, preferred_element_type=F32)
            if h == 0:
                dk_acc[...] = dk
            else:
                dk_acc[...] += dk
            dq_t = lax.dot_general(key_rows, ds, TN, preferred_element_type=F32) * inv_root
            for n in range(2):
                dq[:, cols[n]] = dq_t[:, n * tokens:(n + 1) * tokens].T.astype(BF16)
        if end == group:
            for b in range(window):
                blk = slice(b * tokens, (b + 1) * tokens)
                part[g, 0, b] = (dk_acc[blk] * inv_root).astype(part.dtype)

    half = 4 * tokens

    def product(p, g, n):
        out = jnp.dot(dv_all[head_rows(g), :], slab[p, n], preferred_element_type=F32)
        return out * scale

    def copy1(p, g):
        return remote(out1.at[p, g], in1.at[p, g], send1.at[p, g], recv1.at[p, g], place(PLANS[p][2]))

    def copy2(p, g):
        return remote(out2.at[p, g], in2.at[p, g], send2.at[p, g], recv2.at[p, g], place(PLANS[p][3]))

    def copy3(p):
        return remote(out3.at[p], in3.at[p], send3.at[p], recv3.at[p], place(PLANS[p][2]))

    def first(g):
        all_here(g)
        for p in range(len(PLANS)):
            out1[p, g] = product(p, g, 0).astype(BF16)
            copy1(p, g).start()

    def second(g):
        for p in range(len(PLANS)):
            total = product(p, g, 2)
            copy1(p, g).wait_recv()
            out2[p, g] = (total + in1[p, g].astype(F32)).astype(BF16)
            copy2(p, g).start()

    def aside(g, carry):
        for p in range(len(PLANS)):
            out3[p, g] = product(p, g, 1).astype(BF16)
        return carry

    def third(g, carry):
        for p in range(len(PLANS)):
            total = product(p, g, 3) + in3[p, g].astype(F32)
            copy2(p, g).wait_recv()
            total = total + in2[p, g].astype(F32)
            dw[p * width:(p + 1) * width, head_rows(g)] = total.T
        return carry

    def ready(n):
        for p in range(len(PLANS)):
            hid_wait(p, n)

    def more(n):
        hid_start(0, n, range(7, 0, -1))
        hid_own(0, n).start()

    def attention(g, carry):
        attend(g)
        return carry

    def slot(t, carry):
        @pl.when(t < kv_heads)
        def _():
            finish(t)

        @pl.when(t == 3)
        def _():
            more(1)

        @pl.when((t >= 4) & (t < 4 + kv_heads))
        def _():
            pass_on(t - 4)
            pass_far(t - 4)

            @pl.when(t == 4)
            def _():
                ready(0)

            first(t - 4)

        @pl.when((t >= 8) & (t < 8 + kv_heads))
        def _():
            @pl.when(t == 8)
            def _():
                ready(2)

            second(t - 8)

        @pl.when(t == 8)
        def _():
            more(3)

        @pl.when((t == 0) | (t == 1) | (t == 2) | (t == 9))
        def _():
            g = 1 * (t == 1).astype(jnp.int32) + 2 * (t == 2).astype(jnp.int32) + 3 * (t == 9).astype(jnp.int32)
            descend(g, 0, group)
            part_start(g, 0)

        @pl.when(t == 12)
        def _():
            ready(1)
            lax.fori_loop(0, kv_heads, aside, 0)
            for p in range(len(PLANS)):
                copy3(p).start()

        return carry

    def keys_sum(g, carry):
        close(g)
        return carry

    lax.fori_loop(0, kv_heads, attention, 0)
    lax.fori_loop(0, 13, slot, 0)
    lax.fori_loop(0, kv_heads, keys_sum, 0)
    ready(3)
    for p in range(len(PLANS)):
        copy3(p).wait_recv()
    lax.fori_loop(0, kv_heads, third, 0)

    def sent(g, carry):
        for n in range(2):
            @pl.when(c < 2)
            def _():
                kv_far(g, n).wait_send()

            @pl.when(c != 1)
            def _():
                kv_near(g, n).wait_send()

        for step in range(1, window):
            @pl.when(c >= step)
            def _():
                for n in range(2):
                    part_copy(g, n, step, c - step).wait_send()

        for s in range(4):
            fw_copy(g, s).wait_send()
            if s:
                dv_copy(g, s).wait_send()
        for p in range(len(PLANS)):
            copy1(p, g).wait_send()
            copy2(p, g).wait_send()
        return carry

    lax.fori_loop(0, kv_heads, sent, 0)
    for step in range(1, window):
        @pl.when(c + step < n_ctx)
        def _():
            doc_copy(step, c + step).wait_send()

    for p in range(len(PLANS)):
        copy3(p).wait_send()
        for n in range(4):
            for m in range(1, 8):
                hid_copy(p, n, m).wait_send()


def grouped_call(hidden_in, queries, keys, values, output_gradient, document_index):
    tokens, d = hidden_in.shape
    kv_width = keys.shape[1]
    heads = kv_width // HEAD
    width = d // 32
    plans = len(PLANS)
    span = 3 * tokens
    dma = pltpu.SemaphoreType.DMA
    vmem = pl.BlockSpec(memory_space=pltpu.VMEM)
    hbm = pl.BlockSpec(memory_space=pltpu.HBM)
    return pl.pallas_call(
        grouped,
        out_shape=(
            pltpu.VMEM(queries.shape, BF16),
            pltpu.VMEM(keys.shape, BF16),
            pltpu.VMEM(values.shape, BF16),
            pltpu.VMEM((plans * width, kv_width), F32),
        ),
        in_specs=[hbm] * 6,
        out_specs=(vmem,) * 4,
        scratch_shapes=[
            pltpu.VMEM(queries.shape, BF16),
            pltpu.VMEM(queries.shape, BF16),
            pltpu.VMEM(document_index.shape, jnp.int32),
            pltpu.VMEM((plans, 4, 8 * tokens, width), BF16),
            pltpu.VMEM((heads, 3, 2, tokens, HEAD), BF16),
            pltpu.VMEM((3, 8, tokens), jnp.int32),
            pltpu.VMEM((span, 2 * tokens), F32),
            pltpu.VMEM((heads, queries.shape[1] // (2 * heads * HEAD), span, 2 * tokens), F32),
            pltpu.VMEM((span, HEAD), F32),
            pltpu.VMEM((span, HEAD), F32),
            pltpu.VMEM((heads, 2, 3, tokens, HEAD), BF16),
            pltpu.VMEM((heads, 2, 3, tokens, HEAD), BF16),
            pltpu.VMEM((heads * HEAD, 8 * tokens), BF16),
            pltpu.VMEM((plans, heads, HEAD, width), BF16),
            pltpu.VMEM((plans, heads, HEAD, width), BF16),
            pltpu.VMEM((plans, heads, HEAD, width), BF16),
            pltpu.VMEM((plans, heads, HEAD, width), BF16),
            pltpu.VMEM((plans, heads, HEAD, width), BF16),
            pltpu.VMEM((plans, heads, HEAD, width), BF16),
            dma((3,)), dma((heads, 2)), dma((2, 4)), dma((3,)), dma((3,)),
            dma((heads, 2, 2)), dma((heads, 2, 2)), dma((2, 4, 8)), dma((2, 4, 8)),
            dma((heads, 2, 3)), dma((heads, 2, 3)),
            dma((heads, 6)), dma((heads, 6)), dma((heads, 6)), dma((heads, 6)),
            dma((2, heads)), dma((2, heads)), dma((2, heads)), dma((2, heads)), dma((2,)), dma((2,)),
        ],
        compiler_params=pltpu.CompilerParams(
            collective_id=1, has_side_effects=True, vmem_limit_bytes=58 * 1024 * 1024
        ),
    )(hidden_in, queries, keys, values, output_gradient, document_index)


def store(*refs):
    n = (len(refs) - 1) // 2
    sem = refs[-1]
    copies = [
        pltpu.make_async_copy(a, b, sem.at[i])
        for i, (a, b) in enumerate(zip(refs[:n], refs[n:2 * n]))
    ]
    for copy in copies:
        copy.start()
    for copy in copies:
        copy.wait()


def write_out(*arrays):
    return pl.pallas_call(
        store,
        out_shape=tuple(jax.ShapeDtypeStruct(a.shape, a.dtype) for a in arrays),
        in_specs=[pl.BlockSpec(memory_space=pltpu.VMEM)] * len(arrays),
        out_specs=(pl.BlockSpec(memory_space=pltpu.HBM),) * len(arrays),
        scratch_shapes=[pltpu.SemaphoreType.DMA((len(arrays),))],
        compiler_params=pltpu.CompilerParams(vmem_limit_bytes=8 * 1024 * 1024),
    )(*arrays)


def shards(*arrays):
    sizes = (lax.axis_size("dp"), lax.axis_size("ctx"))
    call = grouped_call if sizes == (8, 4) else general_call
    return write_out(*call(*arrays))


def solution(mesh):
    return jax.shard_map(
        shards,
        mesh=mesh,
        in_specs=(P(("dp", "ctx"), None),) * 5 + (P("dp", "ctx"),),
        out_specs=(P(("dp", "ctx"), None),) * 4,
        check_vma=False,
    )
```

```python
import functools
import math

import jax
import jax.numpy as jnp
from jax import lax
from jax.experimental import pallas as pl
from jax.experimental.pallas import tpu as pltpu
from jax.sharding import PartitionSpec as P

HEAD = 128
MESH = pl.DeviceIdType.MESH
F32 = jnp.float32
BF16 = jnp.bfloat16
NT = (((1,), (1,)), ((), ()))
TN = (((0,), (0,)), ((), ()))


def kernel(
    n_dp, n_ctx, inner,
    hid_hbm, q_hbm, k_hbm, v_hbm, o_hbm, doc_hbm,
    dq, dk_out, dv_out, dw,
    hid, q, o, doc, hid_t, slab, kv, docwin, bias, dk_acc, dv_acc, part, part_in, dv_all,
    y_out, y_in, z_out, z_in,
    load_sem, key_sem, doc_send, doc_recv, kv_send, kv_recv, hid_send, hid_recv, part_send, part_recv,
    dv_send, fw_send, dv_recv, y_send, y_recv, z_send, z_recv,
):
    tokens = q.shape[0]
    width = hid.shape[1]
    outer = n_dp // inner
    chips = n_ctx // 2
    members = inner * 2
    rows = width // (n_dp * n_ctx)
    window = n_ctx // 2 + 1
    last = window - 1
    kv_heads = kv.shape[0]
    group = q.shape[1] // (kv_heads * HEAD)
    inv_root = 1.0 / math.sqrt(HEAD)
    dp = lax.axis_index("dp")
    c = lax.axis_index("ctx")
    far = dp // inner
    near = lax.rem(dp, inner)
    core = lax.rem(c, 2)
    chip = c // 2
    mine = near * 2 + core
    sibling = (dp, c + 1 - 2 * core)

    def member(j):
        return (far * inner + j // 2, chip * 2 + lax.rem(j, 2))

    def across(step):
        return (lax.rem(far + step, outer) * inner + near, c)

    def beside(step):
        return (dp, lax.rem(chip + step, chips) * 2 + core)

    loads = [
        pltpu.make_async_copy(a, b, load_sem.at[n])
        for n, (a, b) in enumerate(((hid_hbm, hid), (q_hbm, q), (o_hbm, o), (doc_hbm, doc)))
    ]
    key_loads = [
        pltpu.make_async_copy(
            ref.at[:, g * HEAD:(g + 1) * HEAD], kv.at[g, last, n], key_sem.at[g, n]
        )
        for g in range(kv_heads) for n, ref in enumerate((k_hbm, v_hbm))
    ]
    loads[3].start()
    for copy in key_loads:
        copy.start()
    for copy in loads[:3]:
        copy.start()

    barrier = pltpu.get_barrier_semaphore()

    def greet(device):
        pl.semaphore_signal(barrier, inc=1, device_id=device, device_id_type=MESH)

    for step in range(1, n_ctx):
        greet((dp, lax.rem(c + step, n_ctx)))
    for step in range(1, members):
        greet(member(lax.rem(mine + step, members)))
    for step in range(1, outer):
        greet(across(step))
    loads[3].wait()
    docwin[last] = jnp.broadcast_to(doc[...], (8, tokens))
    for copy in key_loads:
        copy.wait()
    pl.semaphore_wait(barrier, n_ctx - 1 + members - 1 + outer - 1)

    def doc_copy(step, to):
        return pltpu.make_async_remote_copy(
            src_ref=docwin.at[last], dst_ref=docwin.at[last - step],
            send_sem=doc_send.at[step], recv_sem=doc_recv.at[step],
            device_id=(dp, to), device_id_type=MESH,
        )

    def kv_copy(g, step, to):
        return pltpu.make_async_remote_copy(
            src_ref=kv.at[g, last], dst_ref=kv.at[g, last - step],
            send_sem=kv_send.at[g, step], recv_sem=kv_recv.at[g, step],
            device_id=(dp, to), device_id_type=MESH,
        )

    for step in range(1, window):
        @pl.when(c + step < n_ctx)
        def _():
            doc_copy(step, c + step).start()

    def kv_start(g, carry):
        for step in range(1, window):
            @pl.when(c + step < n_ctx)
            def _():
                kv_copy(g, step, c + step).start()
        return carry

    lax.fori_loop(0, kv_heads, kv_start, 0)

    chunk = 512
    loads[0].wait()

    def turn(n, carry):
        at = pl.multiple_of(n * chunk, chunk)
        hid_t[pl.ds(at, chunk), :] = hid[:, pl.ds(at, chunk)].T
        return carry

    lax.fori_loop(0, width // chunk, turn, 0)

    def rows_of(j, y, z):
        at = ((z * inner + j // 2) * n_ctx + y * 2 + lax.rem(j, 2)) * rows
        return pl.ds(pl.multiple_of(at, rows), rows)

    my_lanes = pl.ds(pl.multiple_of(mine * tokens, tokens), tokens)

    def slab_rows(n):
        return slice(n * rows, (n + 1) * rows)

    def owner_rows(j, n):
        return rows_of(j, lax.rem(chip + n // outer, chips), lax.rem(far + n % outer, outer))

    def hid_copy(step, n):
        j = lax.rem(mine + step, members)
        return pltpu.make_async_remote_copy(
            src_ref=hid_t.at[owner_rows(j, n)],
            dst_ref=slab.at[slab_rows(n), my_lanes],
            send_sem=hid_send.at[n, step], recv_sem=hid_recv.at[n, mine],
            device_id=member(j), device_id_type=MESH,
        )

    blocks = chips * outer
    def hid_start(first, end):
        for n in range(end - 1, first - 1, -1):
            def one(step, carry):
                hid_copy(step, n).start()
                return carry

            lax.fori_loop(1, members, one, 0)

    hid_start(outer, blocks)
    for n in range(blocks):
        slab[slab_rows(n), my_lanes] = hid_t[owner_rows(mine, n)]

    for step in range(1, window):
        @pl.when(c >= step)
        def _():
            doc_copy(step, c).wait_recv()

        @pl.when(c < step)
        def _():
            docwin[last - step] = jnp.full((8, tokens), -1, jnp.int32)
            for g in range(kv_heads):
                kv[g, last - step] = jnp.zeros((2, tokens, HEAD), BF16)

    doc_query = jnp.broadcast_to(doc[...], (tokens, tokens))
    key_row = lax.broadcasted_iota(jnp.int32, (tokens, tokens), 0)
    query_col = lax.broadcasted_iota(jnp.int32, (tokens, tokens), 1)
    for b in range(window):
        doc_key = jnp.broadcast_to(docwin[b][0:1].astype(F32), (tokens, tokens)).T.astype(jnp.int32)
        allowed = doc_key == doc_query
        if b == last:
            allowed = allowed & (key_row <= query_col)
        else:
            allowed = allowed & (doc_key >= 0)
        tile = jnp.where(allowed, 0.0, -1e30)
        bias[b * tokens:(b + 1) * tokens] = jnp.concatenate([tile, tile], axis=1)

    span = window * tokens
    loads[1].wait()
    loads[2].wait()

    def part_copy(g, step, to):
        return pltpu.make_async_remote_copy(
            src_ref=part.at[g, last - step], dst_ref=part_in.at[g, step],
            send_sem=part_send.at[g, step], recv_sem=part_recv.at[g, step],
            device_id=(dp, to), device_id_type=MESH,
        )

    def source(step):
        return 2 * lax.rem(near + inner - step, inner) + core

    def block(j):
        return pl.ds(pl.multiple_of(j * tokens, tokens), tokens)

    def dv_copy(g, step):
        return pltpu.make_async_remote_copy(
            src_ref=dv_all.at[g, block(mine)], dst_ref=dv_all.at[g, block(mine)],
            send_sem=dv_send.at[g, step], recv_sem=dv_recv.at[g, mine],
            device_id=member(2 * lax.rem(near + step, inner) + core), device_id_type=MESH,
        )

    def fw_copy(g, step):
        j = source(step)
        return pltpu.make_async_remote_copy(
            src_ref=dv_all.at[g, block(j)], dst_ref=dv_all.at[g, block(j)],
            send_sem=fw_send.at[g, step], recv_sem=dv_recv.at[g, j],
            device_id=sibling, device_id_type=MESH,
        )

    def arrived(g, j):
        pltpu.make_async_remote_copy(
            src_ref=dv_all.at[g, block(j)], dst_ref=dv_all.at[g, block(j)],
            send_sem=dv_send.at[g, 0], recv_sem=dv_recv.at[g, j],
            device_id=sibling, device_id_type=MESH,
        ).wait_recv()

    def finish(g):
        for step in range(1, window):
            @pl.when(c + step < n_ctx)
            def _():
                part_copy(g, step, c).wait_recv()

            @pl.when(c + step >= n_ctx)
            def _():
                part_in[g, step] = jnp.zeros((2, tokens, HEAD), part_in.dtype)

        cols = pl.ds(pl.multiple_of(g * HEAD, HEAD), HEAD)
        sums = []
        for n in range(2):
            total = part[g, last, n].astype(F32)
            for step in range(1, window):
                total = total + part_in[g, step, n].astype(F32)
            sums.append(total.astype(BF16))
        dk_out[:, cols] = sums[0]
        dv_out[:, cols] = sums[1]
        dv_all[g, block(mine)] = sums[1]
        for step in range(1, inner):
            dv_copy(g, step).start()
        fw_copy(g, 0).start()

    def hid_wait(first, end):
        def one(step, carry):
            j = lax.rem(mine + members - step, members)
            for n in range(first, end):
                pltpu.make_async_remote_copy(
                    src_ref=hid_t.at[pl.ds(0, rows)], dst_ref=slab.at[slab_rows(n), block(j)],
                    send_sem=hid_send.at[n, step], recv_sem=hid_recv.at[n, j],
                    device_id=sibling, device_id_type=MESH,
                ).wait_recv()
            return carry

        lax.fori_loop(1, members, one, 0)

    scale = 1.0 / math.sqrt(tokens * n_dp * n_ctx)

    def product(g, first, end):
        left = slab[first * rows:end * rows, :]
        return jnp.dot(left, dv_all[g], preferred_element_type=F32) * scale

    def y_copy(g, step):
        return pltpu.make_async_remote_copy(
            src_ref=y_out.at[g, step], dst_ref=y_in.at[g, step],
            send_sem=y_send.at[g, step], recv_sem=y_recv.at[g, step],
            device_id=beside(step), device_id_type=MESH,
        )

    def z_copy(g, step):
        return pltpu.make_async_remote_copy(
            src_ref=z_out.at[g, step], dst_ref=z_in.at[g, step],
            send_sem=z_send.at[g, step], recv_sem=z_recv.at[g, step],
            device_id=across(step), device_id_type=MESH,
        )

    def multiply(g, carry):
        for step in range(1, inner):
            arrived(g, source(step))
            fw_copy(g, step).start()
        for step in range(inner):
            arrived(g, source(step) + 1 - 2 * core)
        for step in range(1, chips):
            y_out[g, step] = product(g, step * outer, (step + 1) * outer).astype(BF16)
            y_copy(g, step).start()
        return carry

    def join(g, carry):
        for step in range(1, chips):
            y_copy(g, step).wait_recv()
        for step in range(1, outer):
            total = product(g, step, step + 1)
            for y in range(1, chips):
                total = total + y_in[g, y, slab_rows(step)].astype(F32)
            z_out[g, step] = total.astype(BF16)
            z_copy(g, step).start()
        return carry

    def close(g):
        total = product(g, 0, 1)
        for y in range(1, chips):
            total = total + y_in[g, y, slab_rows(0)].astype(F32)
        for step in range(1, outer):
            z_copy(g, step).wait_recv()
            total = total + z_in[g, step].astype(F32)
        dw[:, pl.ds(pl.multiple_of(g * HEAD, HEAD), HEAD)] = total

    def one_head(g, carry):
        for step in range(1, window):
            @pl.when(c >= step)
            def _():
                kv_copy(g, step, c).wait_recv()

        key_rows = kv[g, :, 0].reshape(span, HEAD)
        value_rows = kv[g, :, 1].reshape(span, HEAD)
        for h in range(0, group, 2):
            at = [pl.ds(pl.multiple_of((g * group + h + n) * HEAD, HEAD), HEAD) for n in range(2)]
            q2 = jnp.concatenate([q[:, at[0]], q[:, at[1]]], axis=0)
            o2 = jnp.concatenate([o[:, at[0]], o[:, at[1]]], axis=0)
            s = lax.dot_general(key_rows, q2, NT, preferred_element_type=F32)
            s = s * inv_root + bias[...]
            e = jnp.exp(s - jnp.max(s, axis=0, keepdims=True))
            p = e * (1.0 / jnp.sum(e, axis=0, keepdims=True))
            t = lax.dot_general(value_rows, o2, NT, preferred_element_type=F32)
            row_dot = jnp.sum(p * t, axis=0, keepdims=True)
            ds = (p * (t - row_dot)).astype(BF16)
            low = p.astype(BF16)
            dk = jnp.dot(ds, q2, preferred_element_type=F32)
            dv = jnp.dot(low, o2, preferred_element_type=F32)
            if h == 0:
                dk_acc[...] = dk
                dv_acc[...] = dv
            else:
                dk_acc[...] += dk
                dv_acc[...] += dv
            dq_t = lax.dot_general(key_rows, ds, TN, preferred_element_type=F32) * inv_root
            for n in range(2):
                dq[:, at[n]] = dq_t[:, n * tokens:(n + 1) * tokens].T.astype(BF16)
        for b in range(window):
            blk = slice(b * tokens, (b + 1) * tokens)
            part[g, b, 0] = (dk_acc[blk] * inv_root).astype(part.dtype)
            part[g, b, 1] = dv_acc[blk].astype(part.dtype)
        for step in range(1, window):
            @pl.when(c >= step)
            def _():
                part_copy(g, step, c - step).start()

        @pl.when(g >= 1)
        def _():
            finish(g - 1)

        return carry

    lax.fori_loop(0, kv_heads, one_head, 0)
    finish(kv_heads - 1)
    hid_start(0, outer)

    hid_wait(outer, blocks)
    lax.fori_loop(0, kv_heads, multiply, 0)
    hid_wait(1, outer)
    lax.fori_loop(0, kv_heads, join, 0)
    hid_wait(0, 1)

    def sent(g, carry):
        close(g)
        for step in range(1, window):
            @pl.when(c + step < n_ctx)
            def _():
                kv_copy(g, step, c + step).wait_send()

            @pl.when(c >= step)
            def _():
                part_copy(g, step, c - step).wait_send()

        for step in range(1, inner):
            dv_copy(g, step).wait_send()
            fw_copy(g, step).wait_send()
        fw_copy(g, 0).wait_send()
        for step in range(1, chips):
            y_copy(g, step).wait_send()
        for step in range(1, outer):
            z_copy(g, step).wait_send()
        return carry

    lax.fori_loop(0, kv_heads, sent, 0)
    for step in range(1, window):
        @pl.when(c + step < n_ctx)
        def _():
            doc_copy(step, c + step).wait_send()

    def hid_sent(step, carry):
        for n in range(blocks):
            hid_copy(step, n).wait_send()
        return carry

    lax.fori_loop(1, members, hid_sent, 0)


def general_call(hidden_in, queries, keys, values, output_gradient, document_index):
    n_dp = lax.axis_size("dp")
    n_ctx = lax.axis_size("ctx")
    tokens, width = hidden_in.shape
    kv_width = keys.shape[1]
    heads = kv_width // HEAD
    inner = min(4, n_dp)
    outer = n_dp // inner
    chips = n_ctx // 2
    members = inner * 2
    rows = width // (n_dp * n_ctx)
    window = n_ctx // 2 + 1
    span = window * tokens
    dma = pltpu.SemaphoreType.DMA
    vmem = pl.BlockSpec(memory_space=pltpu.VMEM)
    hbm = pl.BlockSpec(memory_space=pltpu.HBM)
    return pl.pallas_call(
        functools.partial(kernel, n_dp, n_ctx, inner),
        out_shape=(
            pltpu.VMEM(queries.shape, BF16),
            pltpu.VMEM(keys.shape, BF16),
            pltpu.VMEM(values.shape, BF16),
            pltpu.VMEM((rows, kv_width), F32),
        ),
        in_specs=[hbm] * 6,
        out_specs=(vmem,) * 4,
        scratch_shapes=[
            pltpu.VMEM(hidden_in.shape, BF16),
            pltpu.VMEM(queries.shape, BF16),
            pltpu.VMEM(queries.shape, BF16),
            pltpu.VMEM(document_index.shape, jnp.int32),
            pltpu.VMEM((width, tokens), BF16),
            pltpu.VMEM((chips * outer * rows, members * tokens), BF16),
            pltpu.VMEM((heads, window, 2, tokens, HEAD), BF16),
            pltpu.VMEM((window, 8, tokens), jnp.int32),
            pltpu.VMEM((span, 2 * tokens), F32),
            pltpu.VMEM((span, HEAD), F32),
            pltpu.VMEM((span, HEAD), F32),
            pltpu.VMEM((heads, window, 2, tokens, HEAD), BF16),
            pltpu.VMEM((heads, window, 2, tokens, HEAD), BF16),
            pltpu.VMEM((heads, members * tokens, HEAD), BF16),
            pltpu.VMEM((heads, chips, outer * rows, HEAD), BF16),
            pltpu.VMEM((heads, chips, outer * rows, HEAD), BF16),
            pltpu.VMEM((heads, outer, rows, HEAD), BF16),
            pltpu.VMEM((heads, outer, rows, HEAD), BF16),
            dma((4,)), dma((heads, 2)), dma((window,)), dma((window,)),
            dma((heads, window)), dma((heads, window)),
            dma((chips * outer, members)), dma((chips * outer, members)),
            dma((heads, window)), dma((heads, window)),
            dma((heads, inner)), dma((heads, inner)), dma((heads, members)),
            dma((heads, chips)), dma((heads, chips)),
            dma((heads, outer)), dma((heads, outer)),
        ],
        compiler_params=pltpu.CompilerParams(
            collective_id=0, has_side_effects=True, vmem_limit_bytes=58 * 1024 * 1024
        ),
    )(hidden_in, queries, keys, values, output_gradient, document_index)


DIM = {"x": 1, "l": 2, "h": 4, "y": 2, "k": 1}
PLANS = (("l", "x", "y", "h"),)
CHIPS = ("", "x", "l", "xl")
BLOCKS = ((1, 1), (1, 0), (0, 1), (0, 0))


def grouped(
    hid_hbm, q_hbm, k_hbm, v_hbm, o_hbm, doc_hbm,
    dq, dk_out, dv_out, dw,
    q, o, doc, slab, kv, docwin, bias, probs, dk_acc, dv_acc, part, part_in, dv_all,
    out1, in1, out2, in2, out3, in3,
    load_sem, key_sem, own_sem, doc_send, doc_recv, kv_send, kv_recv, hid_send, hid_recv,
    part_send, part_recv, dv_send, dv_recv, fw_send, fw_recv, send1, recv1, send2, recv2, send3, recv3,
):
    tokens = q.shape[0]
    width = slab.shape[-1]
    window = 3
    last = 2
    n_ctx = 4
    kv_heads = kv.shape[0]
    group = q.shape[1] // (kv_heads * HEAD)
    inv_root = 1.0 / math.sqrt(HEAD)
    scale = 1.0 / math.sqrt(tokens * 32)
    dp = lax.axis_index("dp")
    c = lax.axis_index("ctx")
    at = {"x": lax.rem(dp, 2), "l": lax.rem(dp // 2, 2), "h": dp // 4, "y": c // 2, "k": lax.rem(c, 2)}

    def place(flips):
        p = {d: 1 - at[d] if d in flips else at[d] for d in at}
        return (p["h"] * 4 + p["l"] * 2 + p["x"], p["y"] * 2 + p["k"])

    def remote(src, dst, send, recv, to):
        return pltpu.make_async_remote_copy(
            src_ref=src, dst_ref=dst, send_sem=send, recv_sem=recv,
            device_id=to, device_id_type=MESH,
        )

    loads = [
        pltpu.make_async_copy(a, b, load_sem.at[n])
        for n, (a, b) in enumerate(((q_hbm, q), (o_hbm, o), (doc_hbm, doc)))
    ]
    key_loads = [
        pltpu.make_async_copy(
            ref.at[:, g * HEAD:(g + 1) * HEAD], kv.at[g, last, n], key_sem.at[g, n]
        )
        for g in range(kv_heads) for n, ref in enumerate((k_hbm, v_hbm))
    ]
    loads[2].start()
    for copy in key_loads:
        copy.start()
    for copy in loads[:2]:
        copy.start()

    met = ("k", "y", "yk", "x", "xk", "l", "lk", "xl", "xlk", "xy", "xyk", "h")
    barrier = pltpu.get_barrier_semaphore()
    for flips in met:
        pl.semaphore_signal(barrier, inc=1, device_id=place(flips), device_id_type=MESH)

    def flips_of(dims, bits):
        return "".join(d for d, bit in zip(dims, bits) if bit)

    def hid_pair(p, n, m):
        e, x, r1, r2 = PLANS[p]
        member = flips_of((e, x, "k"), (m // 4, m // 2 % 2, m % 2))
        owner = member + flips_of((r1, r2), BLOCKS[n])
        row, col = place(owner)
        first = pl.multiple_of((row * n_ctx + col) * (len(PLANS) * width) + p * width, width)
        dst = slab.at[p, n, m * tokens:(m + 1) * tokens]
        return member, hid_hbm.at[:, pl.ds(first, width)], dst

    def hid_copy(p, n, m):
        member, src, dst = hid_pair(p, n, m)
        return remote(src, dst, hid_send.at[p, n, m], hid_recv.at[p, n, m], place(member))

    def hid_own(p, n):
        _, src, dst = hid_pair(p, n, 0)
        return pltpu.make_async_copy(src, dst, own_sem.at[p, n])

    def hid_start(p, n, members):
        for m in members:
            hid_copy(p, n, m).start()


    def hid_wait(p, n):
        hid_own(p, n).wait()
        for m in range(1, 8):
            hid_copy(p, n, m).wait_recv()

    loads[2].wait()
    docwin[last] = jnp.broadcast_to(doc[...], (8, tokens))
    for copy in key_loads:
        copy.wait()
    pl.semaphore_wait(barrier, len(met))

    def doc_copy(step, to):
        return remote(docwin.at[last], docwin.at[last - step], doc_send.at[step], doc_recv.at[step], (dp, to))

    def kv_copy(g, n, src, dst, to):
        return remote(kv.at[g, src, n], kv.at[g, dst, n], kv_send.at[g, n, dst], kv_recv.at[g, n, dst], place(to))

    def kv_far(g, n):
        return kv_copy(g, n, last, 0, "y")

    def kv_near(g, n):
        return kv_copy(g, n, last, 1, "k")

    def kv_pass(g, n):
        return kv_copy(g, n, 0, 1, "k")

    for step in range(1, window):
        @pl.when(c + step < n_ctx)
        def _():
            doc_copy(step, c + step).start()

    @pl.when(c < 2)
    def _():
        for n in range(2):
            lax.fori_loop(0, kv_heads, lambda g, carry: (kv_far(g, n).start(), carry)[1], 0)

    @pl.when(lax.rem(c, 2) == 0)
    def _():
        for n in range(2):
            lax.fori_loop(0, kv_heads, lambda g, carry: (kv_near(g, n).start(), carry)[1], 0)

    for n in (0, 2):
        hid_start(0, n, range(7, 0, -1))
        hid_own(0, n).start()

    for step in range(1, window):
        @pl.when(c >= step)
        def _():
            doc_copy(step, c).wait_recv()

        @pl.when(c < step)
        def _():
            docwin[last - step] = jnp.full((8, tokens), -1, jnp.int32)
            for g in range(kv_heads):
                kv[g, last - step] = jnp.zeros((2, tokens, HEAD), BF16)

    doc_query = jnp.broadcast_to(doc[...], (tokens, tokens))
    key_row = lax.broadcasted_iota(jnp.int32, (tokens, tokens), 0)
    query_col = lax.broadcasted_iota(jnp.int32, (tokens, tokens), 1)
    for b in range(window):
        doc_key = jnp.broadcast_to(docwin[b][0:1].astype(F32), (tokens, tokens)).T.astype(jnp.int32)
        allowed = doc_key == doc_query
        if b == last:
            allowed = allowed & (key_row <= query_col)
        else:
            allowed = allowed & (doc_key >= 0)
        tile = jnp.where(allowed, 0.0, -1e30)
        bias[b * tokens:(b + 1) * tokens] = jnp.concatenate([tile, tile], axis=1)

    span = window * tokens
    loads[0].wait()
    loads[1].wait()

    def part_copy(g, n, step, to):
        return remote(
            part.at[g, n, last - step], part_in.at[g, n, step],
            part_send.at[g, n, step], part_recv.at[g, n, step], (dp, to),
        )

    def part_start(g, n):
        for step in range(1, window):
            @pl.when(c >= step)
            def _():
                part_copy(g, n, step, c - step).start()

    def part_sum(g, n):
        for step in range(1, window):
            @pl.when(c + step < n_ctx)
            def _():
                part_copy(g, n, step, c).wait_recv()

            @pl.when(c + step >= n_ctx)
            def _():
                part_in[g, n, step] = jnp.zeros((tokens, HEAD), part_in.dtype)

        total = part[g, n, last].astype(F32)
        for step in range(1, window):
            total = total + part_in[g, n, step].astype(F32)
        return total

    def head_rows(g):
        if isinstance(g, int):
            return slice(g * HEAD, (g + 1) * HEAD)
        return pl.ds(pl.multiple_of(g * HEAD, HEAD), HEAD)

    def lanes(s, core):
        return slice((2 * s + core) * tokens, (2 * s + core + 1) * tokens)

    def dv_copy(g, s):
        rows = head_rows(g)
        return remote(
            dv_all.at[rows, lanes(0, 0)], dv_all.at[rows, lanes(s, 0)],
            dv_send.at[g, s], dv_recv.at[g, s], place(CHIPS[s]),
        )

    def fw_copy(g, s):
        rows = head_rows(g)
        return remote(
            dv_all.at[rows, lanes(s, 0)], dv_all.at[rows, lanes(s, 1)],
            fw_send.at[g, s], fw_recv.at[g, s], place("k"),
        )

    def finish(g):
        total = part_sum(g, 1)
        cols = head_rows(g)
        dv_out[:, cols] = total.astype(BF16)
        dv_all[cols, lanes(0, 0)] = total.T.astype(BF16)
        dv_copy(g, 1).start()
        for s in (3, 2):
            dv_copy(g, s).start()
        fw_copy(g, 0).start()

    def close(g):
        dk_out[:, head_rows(g)] = part_sum(g, 0).astype(BF16)

    def pass_on(g):
        dv_copy(g, 1).wait_recv()
        fw_copy(g, 1).start()
        for s in (2,):
            dv_copy(g, s).wait_recv()
            fw_copy(g, s).start()

    def pass_far(g):
        for s in (3,):
            dv_copy(g, s).wait_recv()
            fw_copy(g, s).start()

    def all_here(g):
        for s in range(4):
            fw_copy(g, s).wait_recv()

    def arrive(g, n):
        @pl.when(c >= 2)
        def _():
            kv_far(g, n).wait_recv()

        @pl.when(c == 3)
        def _():
            kv_pass(g, n).start()

        @pl.when(c >= 1)
        def _():
            kv_near(g, n).wait_recv()

    def two_heads(g, h):
        cols = [pl.ds(pl.multiple_of((g * group + h + n) * HEAD, HEAD), HEAD) for n in range(2)]
        q2 = jnp.concatenate([q[:, cols[0]], q[:, cols[1]]], axis=0)
        o2 = jnp.concatenate([o[:, cols[0]], o[:, cols[1]]], axis=0)
        return cols, q2, o2

    def attend(g):
        arrive(g, 0)
        key_rows = kv[g, :, 0].reshape(span, HEAD)
        for h in range(0, group, 2):
            _, q2, o2 = two_heads(g, h)
            s = lax.dot_general(key_rows, q2, NT, preferred_element_type=F32)
            s = s * inv_root + bias[...]
            e = jnp.exp(s - jnp.max(s, axis=0, keepdims=True))
            p = e * (1.0 / jnp.sum(e, axis=0, keepdims=True))
            probs[g, h // 2] = p
            dv = jnp.dot(p.astype(BF16), o2, preferred_element_type=F32)
            if h == 0:
                dv_acc[...] = dv
            else:
                dv_acc[...] += dv
        for b in range(window):
            part[g, 1, b] = dv_acc[b * tokens:(b + 1) * tokens].astype(part.dtype)
        part_start(g, 1)

    def descend(g, start, end):
        if start == 0:
            arrive(g, 1)
        key_rows = kv[g, :, 0].reshape(span, HEAD)
        value_rows = kv[g, :, 1].reshape(span, HEAD)
        for h in range(start, end, 2):
            cols, q2, o2 = two_heads(g, h)
            p = probs[g, h // 2]
            t = lax.dot_general(value_rows, o2, NT, preferred_element_type=F32)
            row_dot = jnp.sum(p * t, axis=0, keepdims=True)
            ds = (p * (t - row_dot)).astype(BF16)
            dk = jnp.dot(ds, q2, preferred_element_type=F32)
            if h == 0:
                dk_acc[...] = dk
            else:
                dk_acc[...] += dk
            dq_t = lax.dot_general(key_rows, ds, TN, preferred_element_type=F32) * inv_root
            for n in range(2):
                dq[:, cols[n]] = dq_t[:, n * tokens:(n + 1) * tokens].T.astype(BF16)
        if end == group:
            for b in range(window):
                blk = slice(b * tokens, (b + 1) * tokens)
                part[g, 0, b] = (dk_acc[blk] * inv_root).astype(part.dtype)

    half = 4 * tokens

    def product(p, g, n):
        out = jnp.dot(dv_all[head_rows(g), :], slab[p, n], preferred_element_type=F32)
        return out * scale

    def copy1(p, g):
        return remote(out1.at[p, g], in1.at[p, g], send1.at[p, g], recv1.at[p, g], place(PLANS[p][2]))

    def copy2(p, g):
        return remote(out2.at[p, g], in2.at[p, g], send2.at[p, g], recv2.at[p, g], place(PLANS[p][3]))

    def copy3(p):
        return remote(out3.at[p], in3.at[p], send3.at[p], recv3.at[p], place(PLANS[p][2]))

    def first(g):
        all_here(g)
        for p in range(len(PLANS)):
            out1[p, g] = product(p, g, 0).astype(BF16)
            copy1(p, g).start()

    def second(g):
        for p in range(len(PLANS)):
            total = product(p, g, 2)
            copy1(p, g).wait_recv()
            out2[p, g] = (total + in1[p, g].astype(F32)).T.astype(BF16)
            copy2(p, g).start()

    def aside(g, carry):
        for p in range(len(PLANS)):
            out3[p, g] = product(p, g, 1).astype(BF16)
        return carry

    def third(g, carry):
        for p in range(len(PLANS)):
            total = product(p, g, 3) + in3[p, g].astype(F32)
            dw[p * width:(p + 1) * width, head_rows(g)] = total.T
        return carry

    def ending(g, carry):
        for p in range(len(PLANS)):
            copy2(p, g).wait_recv()
            dw[p * width:(p + 1) * width, head_rows(g)] += in2[p, g].astype(F32)
        return carry

    def ready(n):
        for p in range(len(PLANS)):
            hid_wait(p, n)

    def more(n):
        hid_start(0, n, range(7, 0, -1))
        hid_own(0, n).start()

    def attention(g, carry):
        attend(g)
        return carry

    def slot(t, carry):
        @pl.when(t < kv_heads)
        def _():
            finish(t)

        @pl.when(t == 3)
        def _():
            more(1)

        @pl.when((t >= 4) & (t < 4 + kv_heads))
        def _():
            pass_on(t - 4)

        @pl.when((t >= 4) & (t < 4 + kv_heads))
        def _():
            pass_far(t - 4)

        @pl.when((t >= 4) & (t < 4 + kv_heads))
        def _():
            @pl.when(t == 4)
            def _():
                ready(0)

            first(t - 4)

        @pl.when((t >= 8) & (t < 8 + kv_heads))
        def _():
            @pl.when(t == 8)
            def _():
                ready(2)

            second(t - 8)

        @pl.when(t == 8)
        def _():
            hid_start(0, 3, (2, 3, 6, 7))

        @pl.when(t == 11)
        def _():
            hid_start(0, 3, (4, 5, 1))
            hid_own(0, 3).start()

        @pl.when((t == 0) | (t == 1) | (t == 2) | (t == 3))
        def _():
            g = 1 * (t == 1).astype(jnp.int32) + 2 * (t == 2).astype(jnp.int32) + 3 * (t == 3).astype(jnp.int32)
            descend(g, 0, group)
            part_start(g, 0)

        @pl.when(t == 12)
        def _():
            ready(1)
            lax.fori_loop(0, kv_heads, aside, 0)
            for p in range(len(PLANS)):
                copy3(p).start()

        return carry

    def keys_sum(g, carry):
        close(g)
        return carry

    lax.fori_loop(0, kv_heads, attention, 0)
    lax.fori_loop(0, 13, slot, 0)
    lax.fori_loop(0, kv_heads, keys_sum, 0)
    ready(3)
    for p in range(len(PLANS)):
        copy3(p).wait_recv()
    lax.fori_loop(0, kv_heads, third, 0)
    lax.fori_loop(0, kv_heads, ending, 0)

    def sent(g, carry):
        for n in range(2):
            @pl.when(c < 2)
            def _():
                kv_far(g, n).wait_send()

            @pl.when(c != 1)
            def _():
                kv_near(g, n).wait_send()

        for step in range(1, window):
            @pl.when(c >= step)
            def _():
                for n in range(2):
                    part_copy(g, n, step, c - step).wait_send()

        for s in range(4):
            fw_copy(g, s).wait_send()
            if s:
                dv_copy(g, s).wait_send()
        for p in range(len(PLANS)):
            copy1(p, g).wait_send()
            copy2(p, g).wait_send()
        return carry

    lax.fori_loop(0, kv_heads, sent, 0)
    for step in range(1, window):
        @pl.when(c + step < n_ctx)
        def _():
            doc_copy(step, c + step).wait_send()

    for p in range(len(PLANS)):
        copy3(p).wait_send()
        for n in range(4):
            for m in range(1, 8):
                hid_copy(p, n, m).wait_send()


def grouped_call(hidden_in, queries, keys, values, output_gradient, document_index):
    tokens, d = hidden_in.shape
    kv_width = keys.shape[1]
    heads = kv_width // HEAD
    width = d // 32
    plans = len(PLANS)
    span = 3 * tokens
    dma = pltpu.SemaphoreType.DMA
    vmem = pl.BlockSpec(memory_space=pltpu.VMEM)
    hbm = pl.BlockSpec(memory_space=pltpu.HBM)
    return pl.pallas_call(
        grouped,
        out_shape=(
            pltpu.VMEM(queries.shape, BF16),
            pltpu.VMEM(keys.shape, BF16),
            pltpu.VMEM(values.shape, BF16),
            pltpu.VMEM((plans * width, kv_width), F32),
        ),
        in_specs=[hbm] * 6,
        out_specs=(vmem,) * 4,
        scratch_shapes=[
            pltpu.VMEM(queries.shape, BF16),
            pltpu.VMEM(queries.shape, BF16),
            pltpu.VMEM(document_index.shape, jnp.int32),
            pltpu.VMEM((plans, 4, 8 * tokens, width), BF16),
            pltpu.VMEM((heads, 3, 2, tokens, HEAD), BF16),
            pltpu.VMEM((3, 8, tokens), jnp.int32),
            pltpu.VMEM((span, 2 * tokens), F32),
            pltpu.VMEM((heads, queries.shape[1] // (2 * heads * HEAD), span, 2 * tokens), F32),
            pltpu.VMEM((span, HEAD), F32),
            pltpu.VMEM((span, HEAD), F32),
            pltpu.VMEM((heads, 2, 3, tokens, HEAD), BF16),
            pltpu.VMEM((heads, 2, 3, tokens, HEAD), BF16),
            pltpu.VMEM((heads * HEAD, 8 * tokens), BF16),
            pltpu.VMEM((plans, heads, HEAD, width), BF16),
            pltpu.VMEM((plans, heads, HEAD, width), BF16),
            pltpu.VMEM((plans, heads, width, HEAD), BF16),
            pltpu.VMEM((plans, heads, width, HEAD), BF16),
            pltpu.VMEM((plans, heads, HEAD, width), BF16),
            pltpu.VMEM((plans, heads, HEAD, width), BF16),
            dma((3,)), dma((heads, 2)), dma((2, 4)), dma((3,)), dma((3,)),
            dma((heads, 2, 2)), dma((heads, 2, 2)), dma((2, 4, 8)), dma((2, 4, 8)),
            dma((heads, 2, 3)), dma((heads, 2, 3)),
            dma((heads, 6)), dma((heads, 6)), dma((heads, 6)), dma((heads, 6)),
            dma((2, heads)), dma((2, heads)), dma((2, heads)), dma((2, heads)), dma((2,)), dma((2,)),
        ],
        compiler_params=pltpu.CompilerParams(
            collective_id=1, has_side_effects=True, vmem_limit_bytes=58 * 1024 * 1024
        ),
    )(hidden_in, queries, keys, values, output_gradient, document_index)


def store(*refs):
    n = (len(refs) - 1) // 2
    sem = refs[-1]
    copies = [
        pltpu.make_async_copy(a, b, sem.at[i])
        for i, (a, b) in enumerate(zip(refs[:n], refs[n:2 * n]))
    ]
    for copy in copies:
        copy.start()
    for copy in copies:
        copy.wait()


def write_out(*arrays):
    return pl.pallas_call(
        store,
        out_shape=tuple(jax.ShapeDtypeStruct(a.shape, a.dtype) for a in arrays),
        in_specs=[pl.BlockSpec(memory_space=pltpu.VMEM)] * len(arrays),
        out_specs=(pl.BlockSpec(memory_space=pltpu.HBM),) * len(arrays),
        scratch_shapes=[pltpu.SemaphoreType.DMA((len(arrays),))],
        compiler_params=pltpu.CompilerParams(vmem_limit_bytes=8 * 1024 * 1024),
    )(*arrays)


def shards(*arrays):
    sizes = (lax.axis_size("dp"), lax.axis_size("ctx"))
    call = grouped_call if sizes == (8, 4) else general_call
    return write_out(*call(*arrays))


def solution(mesh):
    return jax.shard_map(
        shards,
        mesh=mesh,
        in_specs=(P(("dp", "ctx"), None),) * 5 + (P("dp", "ctx"),),
        out_specs=(P(("dp", "ctx"), None),) * 4,
        check_vma=False,
    )
```

```python
import functools
import math

import jax
import jax.numpy as jnp
from jax import lax
from jax.experimental import pallas as pl
from jax.experimental.pallas import tpu as pltpu
from jax.sharding import PartitionSpec as P

HEAD = 128
MESH = pl.DeviceIdType.MESH
F32 = jnp.float32
BF16 = jnp.bfloat16
NT = (((1,), (1,)), ((), ()))
TN = (((0,), (0,)), ((), ()))


def kernel(
    n_dp, n_ctx, inner,
    hid_hbm, q_hbm, k_hbm, v_hbm, o_hbm, doc_hbm,
    dq, dk_out, dv_out, dw,
    hid, q, o, doc, hid_t, slab, kv, docwin, bias, dk_acc, dv_acc, part, part_in, dv_all,
    y_out, y_in, z_out, z_in,
    load_sem, key_sem, doc_send, doc_recv, kv_send, kv_recv, hid_send, hid_recv, part_send, part_recv,
    dv_send, fw_send, dv_recv, y_send, y_recv, z_send, z_recv,
):
    tokens = q.shape[0]
    width = hid.shape[1]
    outer = n_dp // inner
    chips = n_ctx // 2
    members = inner * 2
    rows = width // (n_dp * n_ctx)
    window = n_ctx // 2 + 1
    last = window - 1
    kv_heads = kv.shape[0]
    group = q.shape[1] // (kv_heads * HEAD)
    inv_root = 1.0 / math.sqrt(HEAD)
    dp = lax.axis_index("dp")
    c = lax.axis_index("ctx")
    far = dp // inner
    near = lax.rem(dp, inner)
    core = lax.rem(c, 2)
    chip = c // 2
    mine = near * 2 + core
    sibling = (dp, c + 1 - 2 * core)

    def member(j):
        return (far * inner + j // 2, chip * 2 + lax.rem(j, 2))

    def across(step):
        return (lax.rem(far + step, outer) * inner + near, c)

    def beside(step):
        return (dp, lax.rem(chip + step, chips) * 2 + core)

    loads = [
        pltpu.make_async_copy(a, b, load_sem.at[n])
        for n, (a, b) in enumerate(((hid_hbm, hid), (q_hbm, q), (o_hbm, o), (doc_hbm, doc)))
    ]
    key_loads = [
        pltpu.make_async_copy(
            ref.at[:, g * HEAD:(g + 1) * HEAD], kv.at[g, last, n], key_sem.at[g, n]
        )
        for g in range(kv_heads) for n, ref in enumerate((k_hbm, v_hbm))
    ]
    loads[3].start()
    for copy in key_loads:
        copy.start()
    for copy in loads[:3]:
        copy.start()

    barrier = pltpu.get_barrier_semaphore()

    def greet(device):
        pl.semaphore_signal(barrier, inc=1, device_id=device, device_id_type=MESH)

    for step in range(1, n_ctx):
        greet((dp, lax.rem(c + step, n_ctx)))
    for step in range(1, members):
        greet(member(lax.rem(mine + step, members)))
    for step in range(1, outer):
        greet(across(step))
    loads[3].wait()
    docwin[last] = jnp.broadcast_to(doc[...], (8, tokens))
    for copy in key_loads:
        copy.wait()
    pl.semaphore_wait(barrier, n_ctx - 1 + members - 1 + outer - 1)

    def doc_copy(step, to):
        return pltpu.make_async_remote_copy(
            src_ref=docwin.at[last], dst_ref=docwin.at[last - step],
            send_sem=doc_send.at[step], recv_sem=doc_recv.at[step],
            device_id=(dp, to), device_id_type=MESH,
        )

    def kv_copy(g, step, to):
        return pltpu.make_async_remote_copy(
            src_ref=kv.at[g, last], dst_ref=kv.at[g, last - step],
            send_sem=kv_send.at[g, step], recv_sem=kv_recv.at[g, step],
            device_id=(dp, to), device_id_type=MESH,
        )

    for step in range(1, window):
        @pl.when(c + step < n_ctx)
        def _():
            doc_copy(step, c + step).start()

    def kv_start(g, carry):
        for step in range(1, window):
            @pl.when(c + step < n_ctx)
            def _():
                kv_copy(g, step, c + step).start()
        return carry

    lax.fori_loop(0, kv_heads, kv_start, 0)

    chunk = 512
    loads[0].wait()

    def turn(n, carry):
        at = pl.multiple_of(n * chunk, chunk)
        hid_t[pl.ds(at, chunk), :] = hid[:, pl.ds(at, chunk)].T
        return carry

    lax.fori_loop(0, width // chunk, turn, 0)

    def rows_of(j, y, z):
        at = ((z * inner + j // 2) * n_ctx + y * 2 + lax.rem(j, 2)) * rows
        return pl.ds(pl.multiple_of(at, rows), rows)

    my_lanes = pl.ds(pl.multiple_of(mine * tokens, tokens), tokens)

    def slab_rows(n):
        return slice(n * rows, (n + 1) * rows)

    def owner_rows(j, n):
        return rows_of(j, lax.rem(chip + n // outer, chips), lax.rem(far + n % outer, outer))

    def hid_copy(step, n):
        j = lax.rem(mine + step, members)
        return pltpu.make_async_remote_copy(
            src_ref=hid_t.at[owner_rows(j, n)],
            dst_ref=slab.at[slab_rows(n), my_lanes],
            send_sem=hid_send.at[n, step], recv_sem=hid_recv.at[n, mine],
            device_id=member(j), device_id_type=MESH,
        )

    blocks = chips * outer
    def hid_start(first, end):
        for n in range(end - 1, first - 1, -1):
            def one(step, carry):
                hid_copy(step, n).start()
                return carry

            lax.fori_loop(1, members, one, 0)

    hid_start(outer, blocks)
    for n in range(blocks):
        slab[slab_rows(n), my_lanes] = hid_t[owner_rows(mine, n)]

    for step in range(1, window):
        @pl.when(c >= step)
        def _():
            doc_copy(step, c).wait_recv()

        @pl.when(c < step)
        def _():
            docwin[last - step] = jnp.full((8, tokens), -1, jnp.int32)
            for g in range(kv_heads):
                kv[g, last - step] = jnp.zeros((2, tokens, HEAD), BF16)

    doc_query = jnp.broadcast_to(doc[...], (tokens, tokens))
    key_row = lax.broadcasted_iota(jnp.int32, (tokens, tokens), 0)
    query_col = lax.broadcasted_iota(jnp.int32, (tokens, tokens), 1)
    for b in range(window):
        doc_key = jnp.broadcast_to(docwin[b][0:1].astype(F32), (tokens, tokens)).T.astype(jnp.int32)
        allowed = doc_key == doc_query
        if b == last:
            allowed = allowed & (key_row <= query_col)
        else:
            allowed = allowed & (doc_key >= 0)
        tile = jnp.where(allowed, 0.0, -1e30)
        bias[b * tokens:(b + 1) * tokens] = jnp.concatenate([tile, tile], axis=1)

    span = window * tokens
    loads[1].wait()
    loads[2].wait()

    def part_copy(g, step, to):
        return pltpu.make_async_remote_copy(
            src_ref=part.at[g, last - step], dst_ref=part_in.at[g, step],
            send_sem=part_send.at[g, step], recv_sem=part_recv.at[g, step],
            device_id=(dp, to), device_id_type=MESH,
        )

    def source(step):
        return 2 * lax.rem(near + inner - step, inner) + core

    def block(j):
        return pl.ds(pl.multiple_of(j * tokens, tokens), tokens)

    def dv_copy(g, step):
        return pltpu.make_async_remote_copy(
            src_ref=dv_all.at[g, block(mine)], dst_ref=dv_all.at[g, block(mine)],
            send_sem=dv_send.at[g, step], recv_sem=dv_recv.at[g, mine],
            device_id=member(2 * lax.rem(near + step, inner) + core), device_id_type=MESH,
        )

    def fw_copy(g, step):
        j = source(step)
        return pltpu.make_async_remote_copy(
            src_ref=dv_all.at[g, block(j)], dst_ref=dv_all.at[g, block(j)],
            send_sem=fw_send.at[g, step], recv_sem=dv_recv.at[g, j],
            device_id=sibling, device_id_type=MESH,
        )

    def arrived(g, j):
        pltpu.make_async_remote_copy(
            src_ref=dv_all.at[g, block(j)], dst_ref=dv_all.at[g, block(j)],
            send_sem=dv_send.at[g, 0], recv_sem=dv_recv.at[g, j],
            device_id=sibling, device_id_type=MESH,
        ).wait_recv()

    def finish(g):
        for step in range(1, window):
            @pl.when(c + step < n_ctx)
            def _():
                part_copy(g, step, c).wait_recv()

            @pl.when(c + step >= n_ctx)
            def _():
                part_in[g, step] = jnp.zeros((2, tokens, HEAD), part_in.dtype)

        cols = pl.ds(pl.multiple_of(g * HEAD, HEAD), HEAD)
        sums = []
        for n in range(2):
            total = part[g, last, n].astype(F32)
            for step in range(1, window):
                total = total + part_in[g, step, n].astype(F32)
            sums.append(total.astype(BF16))
        dk_out[:, cols] = sums[0]
        dv_out[:, cols] = sums[1]
        dv_all[g, block(mine)] = sums[1]
        for step in range(1, inner):
            dv_copy(g, step).start()
        fw_copy(g, 0).start()

    def hid_wait(first, end):
        def one(step, carry):
            j = lax.rem(mine + members - step, members)
            for n in range(first, end):
                pltpu.make_async_remote_copy(
                    src_ref=hid_t.at[pl.ds(0, rows)], dst_ref=slab.at[slab_rows(n), block(j)],
                    send_sem=hid_send.at[n, step], recv_sem=hid_recv.at[n, j],
                    device_id=sibling, device_id_type=MESH,
                ).wait_recv()
            return carry

        lax.fori_loop(1, members, one, 0)

    scale = 1.0 / math.sqrt(tokens * n_dp * n_ctx)

    def product(g, first, end):
        left = slab[first * rows:end * rows, :]
        return jnp.dot(left, dv_all[g], preferred_element_type=F32) * scale

    def y_copy(g, step):
        return pltpu.make_async_remote_copy(
            src_ref=y_out.at[g, step], dst_ref=y_in.at[g, step],
            send_sem=y_send.at[g, step], recv_sem=y_recv.at[g, step],
            device_id=beside(step), device_id_type=MESH,
        )

    def z_copy(g, step):
        return pltpu.make_async_remote_copy(
            src_ref=z_out.at[g, step], dst_ref=z_in.at[g, step],
            send_sem=z_send.at[g, step], recv_sem=z_recv.at[g, step],
            device_id=across(step), device_id_type=MESH,
        )

    def multiply(g, carry):
        for step in range(1, inner):
            arrived(g, source(step))
            fw_copy(g, step).start()
        for step in range(inner):
            arrived(g, source(step) + 1 - 2 * core)
        for step in range(1, chips):
            y_out[g, step] = product(g, step * outer, (step + 1) * outer).astype(BF16)
            y_copy(g, step).start()
        return carry

    def join(g, carry):
        for step in range(1, chips):
            y_copy(g, step).wait_recv()
        for step in range(1, outer):
            total = product(g, step, step + 1)
            for y in range(1, chips):
                total = total + y_in[g, y, slab_rows(step)].astype(F32)
            z_out[g, step] = total.astype(BF16)
            z_copy(g, step).start()
        return carry

    def close(g):
        total = product(g, 0, 1)
        for y in range(1, chips):
            total = total + y_in[g, y, slab_rows(0)].astype(F32)
        for step in range(1, outer):
            z_copy(g, step).wait_recv()
            total = total + z_in[g, step].astype(F32)
        dw[:, pl.ds(pl.multiple_of(g * HEAD, HEAD), HEAD)] = total

    def one_head(g, carry):
        for step in range(1, window):
            @pl.when(c >= step)
            def _():
                kv_copy(g, step, c).wait_recv()

        key_rows = kv[g, :, 0].reshape(span, HEAD)
        value_rows = kv[g, :, 1].reshape(span, HEAD)
        for h in range(0, group, 2):
            at = [pl.ds(pl.multiple_of((g * group + h + n) * HEAD, HEAD), HEAD) for n in range(2)]
            q2 = jnp.concatenate([q[:, at[0]], q[:, at[1]]], axis=0)
            o2 = jnp.concatenate([o[:, at[0]], o[:, at[1]]], axis=0)
            s = lax.dot_general(key_rows, q2, NT, preferred_element_type=F32)
            s = s * inv_root + bias[...]
            e = jnp.exp(s - jnp.max(s, axis=0, keepdims=True))
            p = e * (1.0 / jnp.sum(e, axis=0, keepdims=True))
            t = lax.dot_general(value_rows, o2, NT, preferred_element_type=F32)
            row_dot = jnp.sum(p * t, axis=0, keepdims=True)
            ds = (p * (t - row_dot)).astype(BF16)
            low = p.astype(BF16)
            dk = jnp.dot(ds, q2, preferred_element_type=F32)
            dv = jnp.dot(low, o2, preferred_element_type=F32)
            if h == 0:
                dk_acc[...] = dk
                dv_acc[...] = dv
            else:
                dk_acc[...] += dk
                dv_acc[...] += dv
            dq_t = lax.dot_general(key_rows, ds, TN, preferred_element_type=F32) * inv_root
            for n in range(2):
                dq[:, at[n]] = dq_t[:, n * tokens:(n + 1) * tokens].T.astype(BF16)
        for b in range(window):
            blk = slice(b * tokens, (b + 1) * tokens)
            part[g, b, 0] = (dk_acc[blk] * inv_root).astype(part.dtype)
            part[g, b, 1] = dv_acc[blk].astype(part.dtype)
        for step in range(1, window):
            @pl.when(c >= step)
            def _():
                part_copy(g, step, c - step).start()

        @pl.when(g >= 1)
        def _():
            finish(g - 1)

        return carry

    lax.fori_loop(0, kv_heads, one_head, 0)
    finish(kv_heads - 1)
    hid_start(0, outer)

    hid_wait(outer, blocks)
    lax.fori_loop(0, kv_heads, multiply, 0)
    hid_wait(1, outer)
    lax.fori_loop(0, kv_heads, join, 0)
    hid_wait(0, 1)

    def sent(g, carry):
        close(g)
        for step in range(1, window):
            @pl.when(c + step < n_ctx)
            def _():
                kv_copy(g, step, c + step).wait_send()

            @pl.when(c >= step)
            def _():
                part_copy(g, step, c - step).wait_send()

        for step in range(1, inner):
            dv_copy(g, step).wait_send()
            fw_copy(g, step).wait_send()
        fw_copy(g, 0).wait_send()
        for step in range(1, chips):
            y_copy(g, step).wait_send()
        for step in range(1, outer):
            z_copy(g, step).wait_send()
        return carry

    lax.fori_loop(0, kv_heads, sent, 0)
    for step in range(1, window):
        @pl.when(c + step < n_ctx)
        def _():
            doc_copy(step, c + step).wait_send()

    def hid_sent(step, carry):
        for n in range(blocks):
            hid_copy(step, n).wait_send()
        return carry

    lax.fori_loop(1, members, hid_sent, 0)


def general_call(hidden_in, queries, keys, values, output_gradient, document_index):
    n_dp = lax.axis_size("dp")
    n_ctx = lax.axis_size("ctx")
    tokens, width = hidden_in.shape
    kv_width = keys.shape[1]
    heads = kv_width // HEAD
    inner = min(4, n_dp)
    outer = n_dp // inner
    chips = n_ctx // 2
    members = inner * 2
    rows = width // (n_dp * n_ctx)
    window = n_ctx // 2 + 1
    span = window * tokens
    dma = pltpu.SemaphoreType.DMA
    vmem = pl.BlockSpec(memory_space=pltpu.VMEM)
    hbm = pl.BlockSpec(memory_space=pltpu.HBM)
    return pl.pallas_call(
        functools.partial(kernel, n_dp, n_ctx, inner),
        out_shape=(
            pltpu.VMEM(queries.shape, BF16),
            pltpu.VMEM(keys.shape, BF16),
            pltpu.VMEM(values.shape, BF16),
            pltpu.VMEM((rows, kv_width), F32),
        ),
        in_specs=[hbm] * 6,
        out_specs=(vmem,) * 4,
        scratch_shapes=[
            pltpu.VMEM(hidden_in.shape, BF16),
            pltpu.VMEM(queries.shape, BF16),
            pltpu.VMEM(queries.shape, BF16),
            pltpu.VMEM(document_index.shape, jnp.int32),
            pltpu.VMEM((width, tokens), BF16),
            pltpu.VMEM((chips * outer * rows, members * tokens), BF16),
            pltpu.VMEM((heads, window, 2, tokens, HEAD), BF16),
            pltpu.VMEM((window, 8, tokens), jnp.int32),
            pltpu.VMEM((span, 2 * tokens), F32),
            pltpu.VMEM((span, HEAD), F32),
            pltpu.VMEM((span, HEAD), F32),
            pltpu.VMEM((heads, window, 2, tokens, HEAD), BF16),
            pltpu.VMEM((heads, window, 2, tokens, HEAD), BF16),
            pltpu.VMEM((heads, members * tokens, HEAD), BF16),
            pltpu.VMEM((heads, chips, outer * rows, HEAD), BF16),
            pltpu.VMEM((heads, chips, outer * rows, HEAD), BF16),
            pltpu.VMEM((heads, outer, rows, HEAD), BF16),
            pltpu.VMEM((heads, outer, rows, HEAD), BF16),
            dma((4,)), dma((heads, 2)), dma((window,)), dma((window,)),
            dma((heads, window)), dma((heads, window)),
            dma((chips * outer, members)), dma((chips * outer, members)),
            dma((heads, window)), dma((heads, window)),
            dma((heads, inner)), dma((heads, inner)), dma((heads, members)),
            dma((heads, chips)), dma((heads, chips)),
            dma((heads, outer)), dma((heads, outer)),
        ],
        compiler_params=pltpu.CompilerParams(
            collective_id=0, has_side_effects=True, vmem_limit_bytes=58 * 1024 * 1024
        ),
    )(hidden_in, queries, keys, values, output_gradient, document_index)


DIM = {"x": 1, "l": 2, "h": 4, "y": 2, "k": 1}
PLANS = (("l", "x", "y", "h"),)
CHIPS = ("", "x", "l", "xl")
BLOCKS = ((1, 1), (1, 0), (0, 1), (0, 0))


def grouped(
    hid_hbm, q_hbm, k_hbm, v_hbm, o_hbm, doc_hbm,
    dq, dk_out, dv_out, dw,
    q, o, doc, slab, kv, docwin, bias, probs, dk_acc, dv_acc, part, part_in, dv_all,
    out1, in1, out2, in2, out3, in3,
    load_sem, key_sem, own_sem, doc_send, doc_recv, kv_send, kv_recv, hid_send, hid_recv,
    part_send, part_recv, dv_send, dv_recv, fw_send, fw_recv, send1, recv1, send2, recv2, send3, recv3,
):
    tokens = q.shape[0]
    width = slab.shape[-1]
    window = 3
    last = 2
    n_ctx = 4
    kv_heads = kv.shape[0]
    group = q.shape[1] // (kv_heads * HEAD)
    inv_root = 1.0 / math.sqrt(HEAD)
    scale = 1.0 / math.sqrt(tokens * 32)
    dp = lax.axis_index("dp")
    c = lax.axis_index("ctx")
    at = {"x": lax.rem(dp, 2), "l": lax.rem(dp // 2, 2), "h": dp // 4, "y": c // 2, "k": lax.rem(c, 2)}

    def place(flips):
        p = {d: 1 - at[d] if d in flips else at[d] for d in at}
        return (p["h"] * 4 + p["l"] * 2 + p["x"], p["y"] * 2 + p["k"])

    def remote(src, dst, send, recv, to):
        return pltpu.make_async_remote_copy(
            src_ref=src, dst_ref=dst, send_sem=send, recv_sem=recv,
            device_id=to, device_id_type=MESH,
        )

    loads = [
        pltpu.make_async_copy(a, b, load_sem.at[n])
        for n, (a, b) in enumerate(((q_hbm, q), (o_hbm, o), (doc_hbm, doc)))
    ]
    key_loads = [
        pltpu.make_async_copy(
            ref.at[:, g * HEAD:(g + 1) * HEAD], kv.at[g, last, n], key_sem.at[g, n]
        )
        for g in range(kv_heads) for n, ref in enumerate((k_hbm, v_hbm))
    ]
    loads[2].start()
    for copy in key_loads:
        copy.start()
    for copy in loads[:2]:
        copy.start()

    met = ("k", "y", "yk", "x", "xk", "l", "lk", "xl", "xlk", "h")
    barrier = pltpu.get_barrier_semaphore()
    for flips in met:
        pl.semaphore_signal(barrier, inc=1, device_id=place(flips), device_id_type=MESH)

    def flips_of(dims, bits):
        return "".join(d for d, bit in zip(dims, bits) if bit)

    def hid_pair(p, n, m):
        e, x, r1, r2 = PLANS[p]
        member = flips_of((e, x, "k"), (m // 4, m // 2 % 2, m % 2))
        owner = member + flips_of((r1, r2), BLOCKS[n])
        row, col = place(owner)
        first = pl.multiple_of((row * n_ctx + col) * (len(PLANS) * width) + p * width, width)
        dst = slab.at[p, n, m * tokens:(m + 1) * tokens]
        return member, hid_hbm.at[:, pl.ds(first, width)], dst

    def hid_copy(p, n, m):
        member, src, dst = hid_pair(p, n, m)
        return remote(src, dst, hid_send.at[p, n, m], hid_recv.at[p, n, m], place(member))

    def hid_own(p, n):
        _, src, dst = hid_pair(p, n, 0)
        return pltpu.make_async_copy(src, dst, own_sem.at[p, n])

    def hid_start(p, n, members):
        for m in members:
            hid_copy(p, n, m).start()


    def hid_wait(p, n):
        hid_own(p, n).wait()
        for m in range(1, 8):
            hid_copy(p, n, m).wait_recv()

    loads[2].wait()
    docwin[last] = jnp.broadcast_to(doc[...], (8, tokens))
    for copy in key_loads:
        copy.wait()
    pl.semaphore_wait(barrier, len(met))

    def doc_copy(step, to):
        return remote(docwin.at[last], docwin.at[last - step], doc_send.at[step], doc_recv.at[step], (dp, to))

    def kv_copy(g, n, src, dst, to):
        return remote(kv.at[g, src, n], kv.at[g, dst, n], kv_send.at[g, n, dst], kv_recv.at[g, n, dst], place(to))

    def kv_far(g, n):
        return kv_copy(g, n, last, 0, "y")

    def kv_near(g, n):
        return kv_copy(g, n, last, 1, "k")

    def kv_pass(g, n):
        return kv_copy(g, n, 0, 1, "k")

    for step in range(1, window):
        @pl.when(c + step < n_ctx)
        def _():
            doc_copy(step, c + step).start()

    @pl.when(c < 2)
    def _():
        for n in range(2):
            lax.fori_loop(0, kv_heads, lambda g, carry: (kv_far(g, n).start(), carry)[1], 0)

    @pl.when(lax.rem(c, 2) == 0)
    def _():
        for n in range(2):
            lax.fori_loop(0, kv_heads, lambda g, carry: (kv_near(g, n).start(), carry)[1], 0)

    for n in (0, 2):
        hid_start(0, n, range(7, 0, -1))
        hid_own(0, n).start()

    for step in range(1, window):
        @pl.when(c >= step)
        def _():
            doc_copy(step, c).wait_recv()

        @pl.when(c < step)
        def _():
            docwin[last - step] = jnp.full((8, tokens), -1, jnp.int32)
            for g in range(kv_heads):
                kv[g, last - step] = jnp.zeros((2, tokens, HEAD), BF16)

    doc_query = jnp.broadcast_to(doc[...], (tokens, tokens))
    key_row = lax.broadcasted_iota(jnp.int32, (tokens, tokens), 0)
    query_col = lax.broadcasted_iota(jnp.int32, (tokens, tokens), 1)
    for b in range(window):
        doc_key = jnp.broadcast_to(docwin[b][0:1].astype(F32), (tokens, tokens)).T.astype(jnp.int32)
        allowed = doc_key == doc_query
        if b == last:
            allowed = allowed & (key_row <= query_col)
        else:
            allowed = allowed & (doc_key >= 0)
        tile = jnp.where(allowed, 0.0, -1e30)
        bias[b * tokens:(b + 1) * tokens] = jnp.concatenate([tile, tile], axis=1)

    span = window * tokens
    loads[0].wait()
    loads[1].wait()

    def part_copy(g, n, step, to):
        return remote(
            part.at[g, n, last - step], part_in.at[g, n, step],
            part_send.at[g, n, step], part_recv.at[g, n, step], (dp, to),
        )

    def part_start(g, n):
        for step in range(1, window):
            @pl.when(c >= step)
            def _():
                part_copy(g, n, step, c - step).start()

    def part_sum(g, n):
        for step in range(1, window):
            @pl.when(c + step < n_ctx)
            def _():
                part_copy(g, n, step, c).wait_recv()

            @pl.when(c + step >= n_ctx)
            def _():
                part_in[g, n, step] = jnp.zeros((tokens, HEAD), part_in.dtype)

        total = part[g, n, last].astype(F32)
        for step in range(1, window):
            total = total + part_in[g, n, step].astype(F32)
        return total

    def head_rows(g):
        if isinstance(g, int):
            return slice(g * HEAD, (g + 1) * HEAD)
        return pl.ds(pl.multiple_of(g * HEAD, HEAD), HEAD)

    def lanes(s, core):
        return slice((2 * s + core) * tokens, (2 * s + core + 1) * tokens)

    def dv_copy(g, s):
        rows = head_rows(g)
        return remote(
            dv_all.at[rows, lanes(0, 0)], dv_all.at[rows, lanes(s, 0)],
            dv_send.at[g, s], dv_recv.at[g, s], place(CHIPS[s]),
        )

    def fw_copy(g, s):
        rows = head_rows(g)
        return remote(
            dv_all.at[rows, lanes(s, 0)], dv_all.at[rows, lanes(s, 1)],
            fw_send.at[g, s], fw_recv.at[g, s], place("k"),
        )

    def finish(g):
        total = part_sum(g, 1)
        cols = head_rows(g)
        dv_out[:, cols] = total.astype(BF16)
        dv_all[cols, lanes(0, 0)] = total.T.astype(BF16)
        dv_copy(g, 1).start()
        for s in (3, 2):
            dv_copy(g, s).start()
        fw_copy(g, 0).start()

    def close(g):
        dk_out[:, head_rows(g)] = part_sum(g, 0).astype(BF16)

    def pass_on(g):
        dv_copy(g, 1).wait_recv()
        fw_copy(g, 1).start()
        for s in (2,):
            dv_copy(g, s).wait_recv()
            fw_copy(g, s).start()

    def pass_far(g):
        for s in (3,):
            dv_copy(g, s).wait_recv()
            fw_copy(g, s).start()

    def all_here(g):
        for s in range(4):
            fw_copy(g, s).wait_recv()

    def arrive(g, n):
        @pl.when(c >= 2)
        def _():
            kv_far(g, n).wait_recv()

        @pl.when(c == 3)
        def _():
            kv_pass(g, n).start()

        @pl.when(c >= 1)
        def _():
            kv_near(g, n).wait_recv()

    def two_heads(g, h):
        cols = [pl.ds(pl.multiple_of((g * group + h + n) * HEAD, HEAD), HEAD) for n in range(2)]
        q2 = jnp.concatenate([q[:, cols[0]], q[:, cols[1]]], axis=0)
        o2 = jnp.concatenate([o[:, cols[0]], o[:, cols[1]]], axis=0)
        return cols, q2, o2

    def attend(g):
        arrive(g, 0)
        key_rows = kv[g, :, 0].reshape(span, HEAD)
        for h in range(0, group, 2):
            _, q2, o2 = two_heads(g, h)
            s = lax.dot_general(key_rows, q2, NT, preferred_element_type=F32)
            s = s * inv_root + bias[...]
            e = jnp.exp(s - jnp.max(s, axis=0, keepdims=True))
            p = e * (1.0 / jnp.sum(e, axis=0, keepdims=True))
            probs[g, h // 2] = p
            dv = jnp.dot(p.astype(BF16), o2, preferred_element_type=F32)
            if h == 0:
                dv_acc[...] = dv
            else:
                dv_acc[...] += dv
        for b in range(window):
            part[g, 1, b] = dv_acc[b * tokens:(b + 1) * tokens].astype(part.dtype)
        part_start(g, 1)

    def descend(g, start, end):
        if start == 0:
            arrive(g, 1)
        key_rows = kv[g, :, 0].reshape(span, HEAD)
        value_rows = kv[g, :, 1].reshape(span, HEAD)
        for h in range(start, end, 2):
            cols, q2, o2 = two_heads(g, h)
            p = probs[g, h // 2]
            t = lax.dot_general(value_rows, o2, NT, preferred_element_type=F32)
            row_dot = jnp.sum(p * t, axis=0, keepdims=True)
            ds = (p * (t - row_dot)).astype(BF16)
            dk = jnp.dot(ds, q2, preferred_element_type=F32)
            if h == 0:
                dk_acc[...] = dk
            else:
                dk_acc[...] += dk
            dq_t = lax.dot_general(key_rows, ds, TN, preferred_element_type=F32) * inv_root
            for n in range(2):
                dq[:, cols[n]] = dq_t[:, n * tokens:(n + 1) * tokens].T.astype(BF16)
        if end == group:
            for b in range(window):
                blk = slice(b * tokens, (b + 1) * tokens)
                part[g, 0, b] = (dk_acc[blk] * inv_root).astype(part.dtype)

    half = 4 * tokens

    def product(p, g, n):
        out = jnp.dot(dv_all[head_rows(g), :], slab[p, n], preferred_element_type=F32)
        return out * scale

    def copy1(p, g):
        return remote(out1.at[p, g], in1.at[p, g], send1.at[p, g], recv1.at[p, g], place(PLANS[p][2]))

    def copy2(p, g):
        return remote(out2.at[p, g], in2.at[p, g], send2.at[p, g], recv2.at[p, g], place(PLANS[p][3]))

    def copy3(p):
        return remote(out3.at[p], in3.at[p], send3.at[p], recv3.at[p], place(PLANS[p][2]))

    def first(g):
        all_here(g)
        for p in range(len(PLANS)):
            out1[p, g] = product(p, g, 0).astype(BF16)
            copy1(p, g).start()

    def second(g):
        for p in range(len(PLANS)):
            total = product(p, g, 2)
            copy1(p, g).wait_recv()
            out2[p, g] = (total + in1[p, g].astype(F32)).T.astype(BF16)
            copy2(p, g).start()

    def aside(g, carry):
        for p in range(len(PLANS)):
            out3[p, g] = product(p, g, 1).astype(BF16)
        return carry

    def third(g, carry):
        for p in range(len(PLANS)):
            total = product(p, g, 3) + in3[p, g].astype(F32)
            dw[p * width:(p + 1) * width, head_rows(g)] = total.T
        return carry

    def ending(g, carry):
        for p in range(len(PLANS)):
            copy2(p, g).wait_recv()
            dw[p * width:(p + 1) * width, head_rows(g)] += in2[p, g].astype(F32)
        return carry

    def ready(n):
        for p in range(len(PLANS)):
            hid_wait(p, n)

    def more(n):
        hid_start(0, n, range(7, 0, -1))
        hid_own(0, n).start()

    def attention(g, carry):
        attend(g)
        return carry

    def slot(t, carry):
        @pl.when(t < kv_heads)
        def _():
            finish(t)

        @pl.when(t == 3)
        def _():
            more(1)

        @pl.when((t >= 4) & (t < 4 + kv_heads))
        def _():
            pass_on(t - 4)

        @pl.when((t >= 4) & (t < 4 + kv_heads))
        def _():
            pass_far(t - 4)

        @pl.when((t >= 4) & (t < 4 + kv_heads))
        def _():
            @pl.when(t == 4)
            def _():
                ready(0)

            first(t - 4)

        @pl.when((t >= 8) & (t < 8 + kv_heads))
        def _():
            @pl.when(t == 8)
            def _():
                ready(2)

            second(t - 8)

        @pl.when(t == 8)
        def _():
            hid_start(0, 3, (2, 3, 6, 7))

        @pl.when(t == 11)
        def _():
            hid_start(0, 3, (4, 5, 1))
            hid_own(0, 3).start()

        @pl.when((t == 0) | (t == 1) | (t == 2) | (t == 3))
        def _():
            g = 1 * (t == 1).astype(jnp.int32) + 2 * (t == 2).astype(jnp.int32) + 3 * (t == 3).astype(jnp.int32)
            descend(g, 0, group)
            part_start(g, 0)

        @pl.when(t == 12)
        def _():
            ready(1)
            lax.fori_loop(0, kv_heads, aside, 0)
            for p in range(len(PLANS)):
                copy3(p).start()

        return carry

    def keys_sum(g, carry):
        close(g)
        return carry

    lax.fori_loop(0, kv_heads, attention, 0)
    lax.fori_loop(0, 13, slot, 0)
    lax.fori_loop(0, kv_heads, keys_sum, 0)
    ready(3)
    for p in range(len(PLANS)):
        copy3(p).wait_recv()
    lax.fori_loop(0, kv_heads, third, 0)
    lax.fori_loop(0, kv_heads, ending, 0)

    def sent(g, carry):
        for n in range(2):
            @pl.when(c < 2)
            def _():
                kv_far(g, n).wait_send()

            @pl.when(c != 1)
            def _():
                kv_near(g, n).wait_send()

        for step in range(1, window):
            @pl.when(c >= step)
            def _():
                for n in range(2):
                    part_copy(g, n, step, c - step).wait_send()

        for s in range(4):
            fw_copy(g, s).wait_send()
            if s:
                dv_copy(g, s).wait_send()
        for p in range(len(PLANS)):
            copy1(p, g).wait_send()
            copy2(p, g).wait_send()
        return carry

    lax.fori_loop(0, kv_heads, sent, 0)
    for step in range(1, window):
        @pl.when(c + step < n_ctx)
        def _():
            doc_copy(step, c + step).wait_send()

    for p in range(len(PLANS)):
        copy3(p).wait_send()
        for n in range(4):
            for m in range(1, 8):
                hid_copy(p, n, m).wait_send()


def grouped_call(hidden_in, queries, keys, values, output_gradient, document_index):
    tokens, d = hidden_in.shape
    kv_width = keys.shape[1]
    heads = kv_width // HEAD
    width = d // 32
    plans = len(PLANS)
    span = 3 * tokens
    dma = pltpu.SemaphoreType.DMA
    vmem = pl.BlockSpec(memory_space=pltpu.VMEM)
    hbm = pl.BlockSpec(memory_space=pltpu.HBM)
    return pl.pallas_call(
        grouped,
        out_shape=(
            pltpu.VMEM(queries.shape, BF16),
            pltpu.VMEM(keys.shape, BF16),
            pltpu.VMEM(values.shape, BF16),
            pltpu.VMEM((plans * width, kv_width), F32),
        ),
        in_specs=[hbm] * 6,
        out_specs=(vmem,) * 4,
        scratch_shapes=[
            pltpu.VMEM(queries.shape, BF16),
            pltpu.VMEM(queries.shape, BF16),
            pltpu.VMEM(document_index.shape, jnp.int32),
            pltpu.VMEM((plans, 4, 8 * tokens, width), BF16),
            pltpu.VMEM((heads, 3, 2, tokens, HEAD), BF16),
            pltpu.VMEM((3, 8, tokens), jnp.int32),
            pltpu.VMEM((span, 2 * tokens), F32),
            pltpu.VMEM((heads, queries.shape[1] // (2 * heads * HEAD), span, 2 * tokens), F32),
            pltpu.VMEM((span, HEAD), F32),
            pltpu.VMEM((span, HEAD), F32),
            pltpu.VMEM((heads, 2, 3, tokens, HEAD), BF16),
            pltpu.VMEM((heads, 2, 3, tokens, HEAD), BF16),
            pltpu.VMEM((heads * HEAD, 8 * tokens), BF16),
            pltpu.VMEM((plans, heads, HEAD, width), BF16),
            pltpu.VMEM((plans, heads, HEAD, width), BF16),
            pltpu.VMEM((plans, heads, width, HEAD), BF16),
            pltpu.VMEM((plans, heads, width, HEAD), BF16),
            pltpu.VMEM((plans, heads, HEAD, width), BF16),
            pltpu.VMEM((plans, heads, HEAD, width), BF16),
            dma((3,)), dma((heads, 2)), dma((2, 4)), dma((3,)), dma((3,)),
            dma((heads, 2, 2)), dma((heads, 2, 2)), dma((2, 4, 8)), dma((2, 4, 8)),
            dma((heads, 2, 3)), dma((heads, 2, 3)),
            dma((heads, 6)), dma((heads, 6)), dma((heads, 6)), dma((heads, 6)),
            dma((2, heads)), dma((2, heads)), dma((2, heads)), dma((2, heads)), dma((2,)), dma((2,)),
        ],
        compiler_params=pltpu.CompilerParams(
            collective_id=1, has_side_effects=True, vmem_limit_bytes=58 * 1024 * 1024
        ),
    )(hidden_in, queries, keys, values, output_gradient, document_index)


def store(*refs):
    n = (len(refs) - 1) // 2
    sem = refs[-1]
    copies = [
        pltpu.make_async_copy(a, b, sem.at[i])
        for i, (a, b) in enumerate(zip(refs[:n], refs[n:2 * n]))
    ]
    for copy in copies:
        copy.start()
    for copy in copies:
        copy.wait()


def write_out(*arrays):
    return pl.pallas_call(
        store,
        out_shape=tuple(jax.ShapeDtypeStruct(a.shape, a.dtype) for a in arrays),
        in_specs=[pl.BlockSpec(memory_space=pltpu.VMEM)] * len(arrays),
        out_specs=(pl.BlockSpec(memory_space=pltpu.HBM),) * len(arrays),
        scratch_shapes=[pltpu.SemaphoreType.DMA((len(arrays),))],
        compiler_params=pltpu.CompilerParams(vmem_limit_bytes=8 * 1024 * 1024),
    )(*arrays)


def shards(*arrays):
    sizes = (lax.axis_size("dp"), lax.axis_size("ctx"))
    call = grouped_call if sizes == (8, 4) else general_call
    return write_out(*call(*arrays))


def solution(mesh):
    return jax.shard_map(
        shards,
        mesh=mesh,
        in_specs=(P(("dp", "ctx"), None),) * 5 + (P("dp", "ctx"),),
        out_specs=(P(("dp", "ctx"), None),) * 4,
        check_vma=False,
    )
```

```python
import functools
import math

import jax
import jax.numpy as jnp
from jax import lax
from jax.experimental import pallas as pl
from jax.experimental.pallas import tpu as pltpu
from jax.sharding import PartitionSpec as P

HEAD = 128
MESH = pl.DeviceIdType.MESH
F32 = jnp.float32
BF16 = jnp.bfloat16
NT = (((1,), (1,)), ((), ()))
TN = (((0,), (0,)), ((), ()))


def kernel(
    n_dp, n_ctx, inner,
    hid_hbm, q_hbm, k_hbm, v_hbm, o_hbm, doc_hbm,
    dq, dk_out, dv_out, dw,
    hid, q, o, doc, hid_t, slab, kv, docwin, bias, dk_acc, dv_acc, part, part_in, dv_all,
    y_out, y_in, z_out, z_in,
    load_sem, key_sem, doc_send, doc_recv, kv_send, kv_recv, hid_send, hid_recv, part_send, part_recv,
    dv_send, fw_send, dv_recv, y_send, y_recv, z_send, z_recv,
):
    tokens = q.shape[0]
    width = hid.shape[1]
    outer = n_dp // inner
    chips = n_ctx // 2
    members = inner * 2
    rows = width // (n_dp * n_ctx)
    window = n_ctx // 2 + 1
    last = window - 1
    kv_heads = kv.shape[0]
    group = q.shape[1] // (kv_heads * HEAD)
    inv_root = 1.0 / math.sqrt(HEAD)
    dp = lax.axis_index("dp")
    c = lax.axis_index("ctx")
    far = dp // inner
    near = lax.rem(dp, inner)
    core = lax.rem(c, 2)
    chip = c // 2
    mine = near * 2 + core
    sibling = (dp, c + 1 - 2 * core)

    def member(j):
        return (far * inner + j // 2, chip * 2 + lax.rem(j, 2))

    def across(step):
        return (lax.rem(far + step, outer) * inner + near, c)

    def beside(step):
        return (dp, lax.rem(chip + step, chips) * 2 + core)

    loads = [
        pltpu.make_async_copy(a, b, load_sem.at[n])
        for n, (a, b) in enumerate(((hid_hbm, hid), (q_hbm, q), (o_hbm, o), (doc_hbm, doc)))
    ]
    key_loads = [
        pltpu.make_async_copy(
            ref.at[:, g * HEAD:(g + 1) * HEAD], kv.at[g, last, n], key_sem.at[g, n]
        )
        for g in range(kv_heads) for n, ref in enumerate((k_hbm, v_hbm))
    ]
    loads[3].start()
    for copy in key_loads:
        copy.start()
    for copy in loads[:3]:
        copy.start()

    barrier = pltpu.get_barrier_semaphore()

    def greet(device):
        pl.semaphore_signal(barrier, inc=1, device_id=device, device_id_type=MESH)

    for step in range(1, n_ctx):
        greet((dp, lax.rem(c + step, n_ctx)))
    for step in range(1, members):
        greet(member(lax.rem(mine + step, members)))
    for step in range(1, outer):
        greet(across(step))
    loads[3].wait()
    docwin[last] = jnp.broadcast_to(doc[...], (8, tokens))
    for copy in key_loads:
        copy.wait()
    pl.semaphore_wait(barrier, n_ctx - 1 + members - 1 + outer - 1)

    def doc_copy(step, to):
        return pltpu.make_async_remote_copy(
            src_ref=docwin.at[last], dst_ref=docwin.at[last - step],
            send_sem=doc_send.at[step], recv_sem=doc_recv.at[step],
            device_id=(dp, to), device_id_type=MESH,
        )

    def kv_copy(g, step, to):
        return pltpu.make_async_remote_copy(
            src_ref=kv.at[g, last], dst_ref=kv.at[g, last - step],
            send_sem=kv_send.at[g, step], recv_sem=kv_recv.at[g, step],
            device_id=(dp, to), device_id_type=MESH,
        )

    for step in range(1, window):
        @pl.when(c + step < n_ctx)
        def _():
            doc_copy(step, c + step).start()

    def kv_start(g, carry):
        for step in range(1, window):
            @pl.when(c + step < n_ctx)
            def _():
                kv_copy(g, step, c + step).start()
        return carry

    lax.fori_loop(0, kv_heads, kv_start, 0)

    chunk = 512
    loads[0].wait()

    def turn(n, carry):
        at = pl.multiple_of(n * chunk, chunk)
        hid_t[pl.ds(at, chunk), :] = hid[:, pl.ds(at, chunk)].T
        return carry

    lax.fori_loop(0, width // chunk, turn, 0)

    def rows_of(j, y, z):
        at = ((z * inner + j // 2) * n_ctx + y * 2 + lax.rem(j, 2)) * rows
        return pl.ds(pl.multiple_of(at, rows), rows)

    my_lanes = pl.ds(pl.multiple_of(mine * tokens, tokens), tokens)

    def slab_rows(n):
        return slice(n * rows, (n + 1) * rows)

    def owner_rows(j, n):
        return rows_of(j, lax.rem(chip + n // outer, chips), lax.rem(far + n % outer, outer))

    def hid_copy(step, n):
        j = lax.rem(mine + step, members)
        return pltpu.make_async_remote_copy(
            src_ref=hid_t.at[owner_rows(j, n)],
            dst_ref=slab.at[slab_rows(n), my_lanes],
            send_sem=hid_send.at[n, step], recv_sem=hid_recv.at[n, mine],
            device_id=member(j), device_id_type=MESH,
        )

    blocks = chips * outer
    def hid_start(first, end):
        for n in range(end - 1, first - 1, -1):
            def one(step, carry):
                hid_copy(step, n).start()
                return carry

            lax.fori_loop(1, members, one, 0)

    hid_start(outer, blocks)
    for n in range(blocks):
        slab[slab_rows(n), my_lanes] = hid_t[owner_rows(mine, n)]

    for step in range(1, window):
        @pl.when(c >= step)
        def _():
            doc_copy(step, c).wait_recv()

        @pl.when(c < step)
        def _():
            docwin[last - step] = jnp.full((8, tokens), -1, jnp.int32)
            for g in range(kv_heads):
                kv[g, last - step] = jnp.zeros((2, tokens, HEAD), BF16)

    doc_query = jnp.broadcast_to(doc[...], (tokens, tokens))
    key_row = lax.broadcasted_iota(jnp.int32, (tokens, tokens), 0)
    query_col = lax.broadcasted_iota(jnp.int32, (tokens, tokens), 1)
    for b in range(window):
        doc_key = jnp.broadcast_to(docwin[b][0:1].astype(F32), (tokens, tokens)).T.astype(jnp.int32)
        allowed = doc_key == doc_query
        if b == last:
            allowed = allowed & (key_row <= query_col)
        else:
            allowed = allowed & (doc_key >= 0)
        tile = jnp.where(allowed, 0.0, -1e30)
        bias[b * tokens:(b + 1) * tokens] = jnp.concatenate([tile, tile], axis=1)

    span = window * tokens
    loads[1].wait()
    loads[2].wait()

    def part_copy(g, step, to):
        return pltpu.make_async_remote_copy(
            src_ref=part.at[g, last - step], dst_ref=part_in.at[g, step],
            send_sem=part_send.at[g, step], recv_sem=part_recv.at[g, step],
            device_id=(dp, to), device_id_type=MESH,
        )

    def source(step):
        return 2 * lax.rem(near + inner - step, inner) + core

    def block(j):
        return pl.ds(pl.multiple_of(j * tokens, tokens), tokens)

    def dv_copy(g, step):
        return pltpu.make_async_remote_copy(
            src_ref=dv_all.at[g, block(mine)], dst_ref=dv_all.at[g, block(mine)],
            send_sem=dv_send.at[g, step], recv_sem=dv_recv.at[g, mine],
            device_id=member(2 * lax.rem(near + step, inner) + core), device_id_type=MESH,
        )

    def fw_copy(g, step):
        j = source(step)
        return pltpu.make_async_remote_copy(
            src_ref=dv_all.at[g, block(j)], dst_ref=dv_all.at[g, block(j)],
            send_sem=fw_send.at[g, step], recv_sem=dv_recv.at[g, j],
            device_id=sibling, device_id_type=MESH,
        )

    def arrived(g, j):
        pltpu.make_async_remote_copy(
            src_ref=dv_all.at[g, block(j)], dst_ref=dv_all.at[g, block(j)],
            send_sem=dv_send.at[g, 0], recv_sem=dv_recv.at[g, j],
            device_id=sibling, device_id_type=MESH,
        ).wait_recv()

    def finish(g):
        for step in range(1, window):
            @pl.when(c + step < n_ctx)
            def _():
                part_copy(g, step, c).wait_recv()

            @pl.when(c + step >= n_ctx)
            def _():
                part_in[g, step] = jnp.zeros((2, tokens, HEAD), part_in.dtype)

        cols = pl.ds(pl.multiple_of(g * HEAD, HEAD), HEAD)
        sums = []
        for n in range(2):
            total = part[g, last, n].astype(F32)
            for step in range(1, window):
                total = total + part_in[g, step, n].astype(F32)
            sums.append(total.astype(BF16))
        dk_out[:, cols] = sums[0]
        dv_out[:, cols] = sums[1]
        dv_all[g, block(mine)] = sums[1]
        for step in range(1, inner):
            dv_copy(g, step).start()
        fw_copy(g, 0).start()

    def hid_wait(first, end):
        def one(step, carry):
            j = lax.rem(mine + members - step, members)
            for n in range(first, end):
                pltpu.make_async_remote_copy(
                    src_ref=hid_t.at[pl.ds(0, rows)], dst_ref=slab.at[slab_rows(n), block(j)],
                    send_sem=hid_send.at[n, step], recv_sem=hid_recv.at[n, j],
                    device_id=sibling, device_id_type=MESH,
                ).wait_recv()
            return carry

        lax.fori_loop(1, members, one, 0)

    scale = 1.0 / math.sqrt(tokens * n_dp * n_ctx)

    def product(g, first, end):
        left = slab[first * rows:end * rows, :]
        return jnp.dot(left, dv_all[g], preferred_element_type=F32) * scale

    def y_copy(g, step):
        return pltpu.make_async_remote_copy(
            src_ref=y_out.at[g, step], dst_ref=y_in.at[g, step],
            send_sem=y_send.at[g, step], recv_sem=y_recv.at[g, step],
            device_id=beside(step), device_id_type=MESH,
        )

    def z_copy(g, step):
        return pltpu.make_async_remote_copy(
            src_ref=z_out.at[g, step], dst_ref=z_in.at[g, step],
            send_sem=z_send.at[g, step], recv_sem=z_recv.at[g, step],
            device_id=across(step), device_id_type=MESH,
        )

    def multiply(g, carry):
        for step in range(1, inner):
            arrived(g, source(step))
            fw_copy(g, step).start()
        for step in range(inner):
            arrived(g, source(step) + 1 - 2 * core)
        for step in range(1, chips):
            y_out[g, step] = product(g, step * outer, (step + 1) * outer).astype(BF16)
            y_copy(g, step).start()
        return carry

    def join(g, carry):
        for step in range(1, chips):
            y_copy(g, step).wait_recv()
        for step in range(1, outer):
            total = product(g, step, step + 1)
            for y in range(1, chips):
                total = total + y_in[g, y, slab_rows(step)].astype(F32)
            z_out[g, step] = total.astype(BF16)
            z_copy(g, step).start()
        return carry

    def close(g):
        total = product(g, 0, 1)
        for y in range(1, chips):
            total = total + y_in[g, y, slab_rows(0)].astype(F32)
        for step in range(1, outer):
            z_copy(g, step).wait_recv()
            total = total + z_in[g, step].astype(F32)
        dw[:, pl.ds(pl.multiple_of(g * HEAD, HEAD), HEAD)] = total

    def one_head(g, carry):
        for step in range(1, window):
            @pl.when(c >= step)
            def _():
                kv_copy(g, step, c).wait_recv()

        key_rows = kv[g, :, 0].reshape(span, HEAD)
        value_rows = kv[g, :, 1].reshape(span, HEAD)
        for h in range(0, group, 2):
            at = [pl.ds(pl.multiple_of((g * group + h + n) * HEAD, HEAD), HEAD) for n in range(2)]
            q2 = jnp.concatenate([q[:, at[0]], q[:, at[1]]], axis=0)
            o2 = jnp.concatenate([o[:, at[0]], o[:, at[1]]], axis=0)
            s = lax.dot_general(key_rows, q2, NT, preferred_element_type=F32)
            s = s * inv_root + bias[...]
            e = jnp.exp(s - jnp.max(s, axis=0, keepdims=True))
            p = e * (1.0 / jnp.sum(e, axis=0, keepdims=True))
            t = lax.dot_general(value_rows, o2, NT, preferred_element_type=F32)
            row_dot = jnp.sum(p * t, axis=0, keepdims=True)
            ds = (p * (t - row_dot)).astype(BF16)
            low = p.astype(BF16)
            dk = jnp.dot(ds, q2, preferred_element_type=F32)
            dv = jnp.dot(low, o2, preferred_element_type=F32)
            if h == 0:
                dk_acc[...] = dk
                dv_acc[...] = dv
            else:
                dk_acc[...] += dk
                dv_acc[...] += dv
            dq_t = lax.dot_general(key_rows, ds, TN, preferred_element_type=F32) * inv_root
            for n in range(2):
                dq[:, at[n]] = dq_t[:, n * tokens:(n + 1) * tokens].T.astype(BF16)
        for b in range(window):
            blk = slice(b * tokens, (b + 1) * tokens)
            part[g, b, 0] = (dk_acc[blk] * inv_root).astype(part.dtype)
            part[g, b, 1] = dv_acc[blk].astype(part.dtype)
        for step in range(1, window):
            @pl.when(c >= step)
            def _():
                part_copy(g, step, c - step).start()

        @pl.when(g >= 1)
        def _():
            finish(g - 1)

        return carry

    lax.fori_loop(0, kv_heads, one_head, 0)
    finish(kv_heads - 1)
    hid_start(0, outer)

    hid_wait(outer, blocks)
    lax.fori_loop(0, kv_heads, multiply, 0)
    hid_wait(1, outer)
    lax.fori_loop(0, kv_heads, join, 0)
    hid_wait(0, 1)

    def sent(g, carry):
        close(g)
        for step in range(1, window):
            @pl.when(c + step < n_ctx)
            def _():
                kv_copy(g, step, c + step).wait_send()

            @pl.when(c >= step)
            def _():
                part_copy(g, step, c - step).wait_send()

        for step in range(1, inner):
            dv_copy(g, step).wait_send()
            fw_copy(g, step).wait_send()
        fw_copy(g, 0).wait_send()
        for step in range(1, chips):
            y_copy(g, step).wait_send()
        for step in range(1, outer):
            z_copy(g, step).wait_send()
        return carry

    lax.fori_loop(0, kv_heads, sent, 0)
    for step in range(1, window):
        @pl.when(c + step < n_ctx)
        def _():
            doc_copy(step, c + step).wait_send()

    def hid_sent(step, carry):
        for n in range(blocks):
            hid_copy(step, n).wait_send()
        return carry

    lax.fori_loop(1, members, hid_sent, 0)


def general_call(hidden_in, queries, keys, values, output_gradient, document_index):
    n_dp = lax.axis_size("dp")
    n_ctx = lax.axis_size("ctx")
    tokens, width = hidden_in.shape
    kv_width = keys.shape[1]
    heads = kv_width // HEAD
    inner = min(4, n_dp)
    outer = n_dp // inner
    chips = n_ctx // 2
    members = inner * 2
    rows = width // (n_dp * n_ctx)
    window = n_ctx // 2 + 1
    span = window * tokens
    dma = pltpu.SemaphoreType.DMA
    vmem = pl.BlockSpec(memory_space=pltpu.VMEM)
    hbm = pl.BlockSpec(memory_space=pltpu.HBM)
    return pl.pallas_call(
        functools.partial(kernel, n_dp, n_ctx, inner),
        out_shape=(
            pltpu.VMEM(queries.shape, BF16),
            pltpu.VMEM(keys.shape, BF16),
            pltpu.VMEM(values.shape, BF16),
            pltpu.VMEM((rows, kv_width), F32),
        ),
        in_specs=[hbm] * 6,
        out_specs=(vmem,) * 4,
        scratch_shapes=[
            pltpu.VMEM(hidden_in.shape, BF16),
            pltpu.VMEM(queries.shape, BF16),
            pltpu.VMEM(queries.shape, BF16),
            pltpu.VMEM(document_index.shape, jnp.int32),
            pltpu.VMEM((width, tokens), BF16),
            pltpu.VMEM((chips * outer * rows, members * tokens), BF16),
            pltpu.VMEM((heads, window, 2, tokens, HEAD), BF16),
            pltpu.VMEM((window, 8, tokens), jnp.int32),
            pltpu.VMEM((span, 2 * tokens), F32),
            pltpu.VMEM((span, HEAD), F32),
            pltpu.VMEM((span, HEAD), F32),
            pltpu.VMEM((heads, window, 2, tokens, HEAD), BF16),
            pltpu.VMEM((heads, window, 2, tokens, HEAD), BF16),
            pltpu.VMEM((heads, members * tokens, HEAD), BF16),
            pltpu.VMEM((heads, chips, outer * rows, HEAD), BF16),
            pltpu.VMEM((heads, chips, outer * rows, HEAD), BF16),
            pltpu.VMEM((heads, outer, rows, HEAD), BF16),
            pltpu.VMEM((heads, outer, rows, HEAD), BF16),
            dma((4,)), dma((heads, 2)), dma((window,)), dma((window,)),
            dma((heads, window)), dma((heads, window)),
            dma((chips * outer, members)), dma((chips * outer, members)),
            dma((heads, window)), dma((heads, window)),
            dma((heads, inner)), dma((heads, inner)), dma((heads, members)),
            dma((heads, chips)), dma((heads, chips)),
            dma((heads, outer)), dma((heads, outer)),
        ],
        compiler_params=pltpu.CompilerParams(
            collective_id=0, has_side_effects=True, vmem_limit_bytes=58 * 1024 * 1024
        ),
    )(hidden_in, queries, keys, values, output_gradient, document_index)


DIM = {"x": 1, "l": 2, "h": 4, "y": 2, "k": 1}
PLANS = (("l", "x", "y", "h"),)
CHIPS = ("", "x", "l", "xl")
BLOCKS = ((1, 1), (1, 0), (0, 1), (0, 0))


def grouped(
    hid_hbm, q_hbm, k_hbm, v_hbm, o_hbm, doc_hbm,
    dq, dk_out, dv_out, dw,
    q, o, doc, slab, kv, docwin, bias, probs, dk_acc, dv_acc, part, part_in, dv_all,
    out1, in1, out2, in2, out3, in3,
    load_sem, key_sem, own_sem, doc_send, doc_recv, kv_send, kv_recv, hid_send, hid_recv,
    part_send, part_recv, dv_send, dv_recv, fw_send, fw_recv, send1, recv1, send2, recv2, send3, recv3,
):
    tokens = q.shape[0]
    width = slab.shape[-1]
    window = 3
    last = 2
    n_ctx = 4
    kv_heads = kv.shape[0]
    group = q.shape[1] // (kv_heads * HEAD)
    inv_root = 1.0 / math.sqrt(HEAD)
    scale = 1.0 / math.sqrt(tokens * 32)
    dp = lax.axis_index("dp")
    c = lax.axis_index("ctx")
    at = {"x": lax.rem(dp, 2), "l": lax.rem(dp // 2, 2), "h": dp // 4, "y": c // 2, "k": lax.rem(c, 2)}

    def place(flips):
        p = {d: 1 - at[d] if d in flips else at[d] for d in at}
        return (p["h"] * 4 + p["l"] * 2 + p["x"], p["y"] * 2 + p["k"])

    def remote(src, dst, send, recv, to):
        return pltpu.make_async_remote_copy(
            src_ref=src, dst_ref=dst, send_sem=send, recv_sem=recv,
            device_id=to, device_id_type=MESH,
        )

    loads = [
        pltpu.make_async_copy(a, b, load_sem.at[n])
        for n, (a, b) in enumerate(((q_hbm, q), (o_hbm, o), (doc_hbm, doc)))
    ]
    key_loads = [
        pltpu.make_async_copy(
            ref.at[:, g * HEAD:(g + 1) * HEAD], kv.at[g, last, n], key_sem.at[g, n]
        )
        for g in range(kv_heads) for n, ref in enumerate((k_hbm, v_hbm))
    ]
    loads[2].start()
    for copy in key_loads:
        copy.start()
    for copy in loads[:2]:
        copy.start()

    met = ("h", "xl", "xlk", "x", "xk", "l", "lk", "y", "yk", "k")
    barrier = pltpu.get_barrier_semaphore()
    for flips in met:
        pl.semaphore_signal(barrier, inc=1, device_id=place(flips), device_id_type=MESH)

    def flips_of(dims, bits):
        return "".join(d for d, bit in zip(dims, bits) if bit)

    def hid_pair(p, n, m):
        e, x, r1, r2 = PLANS[p]
        member = flips_of((e, x, "k"), (m // 4, m // 2 % 2, m % 2))
        owner = member + flips_of((r1, r2), BLOCKS[n])
        row, col = place(owner)
        first = pl.multiple_of((row * n_ctx + col) * (len(PLANS) * width) + p * width, width)
        dst = slab.at[p, n, m * tokens:(m + 1) * tokens]
        return member, hid_hbm.at[:, pl.ds(first, width)], dst

    def hid_copy(p, n, m):
        member, src, dst = hid_pair(p, n, m)
        return remote(src, dst, hid_send.at[p, n, m], hid_recv.at[p, n, m], place(member))

    def hid_own(p, n):
        _, src, dst = hid_pair(p, n, 0)
        return pltpu.make_async_copy(src, dst, own_sem.at[p, n])

    def hid_start(p, n, members):
        for m in members:
            hid_copy(p, n, m).start()


    def hid_wait(p, n):
        hid_own(p, n).wait()
        for m in range(1, 8):
            hid_copy(p, n, m).wait_recv()

    loads[2].wait()
    docwin[last] = jnp.broadcast_to(doc[...], (8, tokens))
    for copy in key_loads:
        copy.wait()
    pl.semaphore_wait(barrier, len(met))

    def doc_copy(step, to):
        return remote(docwin.at[last], docwin.at[last - step], doc_send.at[step], doc_recv.at[step], (dp, to))

    def kv_copy(g, n, src, dst, to):
        return remote(kv.at[g, src, n], kv.at[g, dst, n], kv_send.at[g, n, dst], kv_recv.at[g, n, dst], place(to))

    def kv_far(g, n):
        return kv_copy(g, n, last, 0, "y")

    def kv_near(g, n):
        return kv_copy(g, n, last, 1, "k")

    def kv_pass(g, n):
        return kv_copy(g, n, 0, 1, "k")

    for step in range(1, window):
        @pl.when(c + step < n_ctx)
        def _():
            doc_copy(step, c + step).start()

    @pl.when(c < 2)
    def _():
        for n in range(2):
            lax.fori_loop(0, kv_heads, lambda g, carry: (kv_far(g, n).start(), carry)[1], 0)

    @pl.when(lax.rem(c, 2) == 0)
    def _():
        for n in range(2):
            lax.fori_loop(0, kv_heads, lambda g, carry: (kv_near(g, n).start(), carry)[1], 0)

    for n in (0, 2):
        hid_start(0, n, range(7, 0, -1))
        hid_own(0, n).start()

    for step in range(1, window):
        @pl.when(c >= step)
        def _():
            doc_copy(step, c).wait_recv()

        @pl.when(c < step)
        def _():
            docwin[last - step] = jnp.full((8, tokens), -1, jnp.int32)
            for g in range(kv_heads):
                kv[g, last - step] = jnp.zeros((2, tokens, HEAD), BF16)

    doc_query = jnp.broadcast_to(doc[...], (tokens, tokens))
    key_row = lax.broadcasted_iota(jnp.int32, (tokens, tokens), 0)
    query_col = lax.broadcasted_iota(jnp.int32, (tokens, tokens), 1)
    for b in range(window):
        doc_key = jnp.broadcast_to(docwin[b][0:1].astype(F32), (tokens, tokens)).T.astype(jnp.int32)
        allowed = doc_key == doc_query
        if b == last:
            allowed = allowed & (key_row <= query_col)
        else:
            allowed = allowed & (doc_key >= 0)
        tile = jnp.where(allowed, 0.0, -1e30)
        bias[b * tokens:(b + 1) * tokens] = jnp.concatenate([tile, tile], axis=1)

    span = window * tokens
    loads[0].wait()
    loads[1].wait()

    def part_copy(g, n, step, to):
        return remote(
            part.at[g, n, last - step], part_in.at[g, n, step],
            part_send.at[g, n, step], part_recv.at[g, n, step], (dp, to),
        )

    def part_start(g, n):
        for step in range(1, window):
            @pl.when(c >= step)
            def _():
                part_copy(g, n, step, c - step).start()

    def part_sum(g, n):
        for step in range(1, window):
            @pl.when(c + step < n_ctx)
            def _():
                part_copy(g, n, step, c).wait_recv()

            @pl.when(c + step >= n_ctx)
            def _():
                part_in[g, n, step] = jnp.zeros((tokens, HEAD), part_in.dtype)

        total = part[g, n, last].astype(F32)
        for step in range(1, window):
            total = total + part_in[g, n, step].astype(F32)
        return total

    def head_rows(g):
        if isinstance(g, int):
            return slice(g * HEAD, (g + 1) * HEAD)
        return pl.ds(pl.multiple_of(g * HEAD, HEAD), HEAD)

    def lanes(s, core):
        return slice((2 * s + core) * tokens, (2 * s + core + 1) * tokens)

    def dv_copy(g, s):
        rows = head_rows(g)
        return remote(
            dv_all.at[rows, lanes(0, 0)], dv_all.at[rows, lanes(s, 0)],
            dv_send.at[g, s], dv_recv.at[g, s], place(CHIPS[s]),
        )

    def fw_copy(g, s):
        rows = head_rows(g)
        return remote(
            dv_all.at[rows, lanes(s, 0)], dv_all.at[rows, lanes(s, 1)],
            fw_send.at[g, s], fw_recv.at[g, s], place("k"),
        )

    def finish(g):
        total = part_sum(g, 1)
        cols = head_rows(g)
        dv_out[:, cols] = total.astype(BF16)
        dv_all[cols, lanes(0, 0)] = total.T.astype(BF16)
        dv_copy(g, 1).start()
        for s in (3, 2):
            dv_copy(g, s).start()
        fw_copy(g, 0).start()

    def close(g):
        dk_out[:, head_rows(g)] = part_sum(g, 0).astype(BF16)

    def pass_on(g):
        dv_copy(g, 1).wait_recv()
        fw_copy(g, 1).start()
        for s in (2,):
            dv_copy(g, s).wait_recv()
            fw_copy(g, s).start()

    def pass_far(g):
        for s in (3,):
            dv_copy(g, s).wait_recv()
            fw_copy(g, s).start()

    def all_here(g):
        for s in range(4):
            fw_copy(g, s).wait_recv()

    def arrive(g, n):
        @pl.when(c >= 2)
        def _():
            kv_far(g, n).wait_recv()

        @pl.when(c == 3)
        def _():
            kv_pass(g, n).start()

        @pl.when(c >= 1)
        def _():
            kv_near(g, n).wait_recv()

    def two_heads(g, h):
        cols = [pl.ds(pl.multiple_of((g * group + h + n) * HEAD, HEAD), HEAD) for n in range(2)]
        q2 = jnp.concatenate([q[:, cols[0]], q[:, cols[1]]], axis=0)
        o2 = jnp.concatenate([o[:, cols[0]], o[:, cols[1]]], axis=0)
        return cols, q2, o2

    def attend(g):
        arrive(g, 0)
        key_rows = kv[g, :, 0].reshape(span, HEAD)
        for h in range(0, group, 2):
            _, q2, o2 = two_heads(g, h)
            s = lax.dot_general(key_rows, q2, NT, preferred_element_type=F32)
            s = s * inv_root + bias[...]
            e = jnp.exp(s - jnp.max(s, axis=0, keepdims=True))
            p = e * (1.0 / jnp.sum(e, axis=0, keepdims=True))
            probs[g, h // 2] = p
            dv = jnp.dot(p.astype(BF16), o2, preferred_element_type=F32)
            if h == 0:
                dv_acc[...] = dv
            else:
                dv_acc[...] += dv
        for b in range(window):
            part[g, 1, b] = dv_acc[b * tokens:(b + 1) * tokens].astype(part.dtype)
        part_start(g, 1)

    def descend(g, start, end):
        if start == 0:
            arrive(g, 1)
        key_rows = kv[g, :, 0].reshape(span, HEAD)
        value_rows = kv[g, :, 1].reshape(span, HEAD)
        for h in range(start, end, 2):
            cols, q2, o2 = two_heads(g, h)
            p = probs[g, h // 2]
            t = lax.dot_general(value_rows, o2, NT, preferred_element_type=F32)
            row_dot = jnp.sum(p * t, axis=0, keepdims=True)
            ds = (p * (t - row_dot)).astype(BF16)
            dk = jnp.dot(ds, q2, preferred_element_type=F32)
            if h == 0:
                dk_acc[...] = dk
            else:
                dk_acc[...] += dk
            dq_t = lax.dot_general(key_rows, ds, TN, preferred_element_type=F32) * inv_root
            for n in range(2):
                dq[:, cols[n]] = dq_t[:, n * tokens:(n + 1) * tokens].T.astype(BF16)
        if end == group:
            for b in range(window):
                blk = slice(b * tokens, (b + 1) * tokens)
                part[g, 0, b] = (dk_acc[blk] * inv_root).astype(part.dtype)

    half = 4 * tokens

    def product(p, g, n):
        out = jnp.dot(dv_all[head_rows(g), :], slab[p, n], preferred_element_type=F32)
        return out * scale

    def copy1(p, g):
        return remote(out1.at[p, g], in1.at[p, g], send1.at[p, g], recv1.at[p, g], place(PLANS[p][2]))

    def copy2(p, g):
        return remote(out2.at[p, g], in2.at[p, g], send2.at[p, g], recv2.at[p, g], place(PLANS[p][3]))

    def copy3(p):
        return remote(out3.at[p], in3.at[p], send3.at[p], recv3.at[p], place(PLANS[p][2]))

    def first(g):
        all_here(g)
        for p in range(len(PLANS)):
            out1[p, g] = product(p, g, 0).astype(BF16)
            copy1(p, g).start()

    def second(g):
        for p in range(len(PLANS)):
            total = product(p, g, 2)
            copy1(p, g).wait_recv()
            out2[p, g] = (total + in1[p, g].astype(F32)).T.astype(BF16)
            copy2(p, g).start()

    def aside(g, carry):
        for p in range(len(PLANS)):
            out3[p, g] = product(p, g, 1).astype(BF16)
        return carry

    def third(g, carry):
        for p in range(len(PLANS)):
            total = product(p, g, 3) + in3[p, g].astype(F32)
            dw[p * width:(p + 1) * width, head_rows(g)] = total.T
        return carry

    def ending(g, carry):
        for p in range(len(PLANS)):
            copy2(p, g).wait_recv()
            dw[p * width:(p + 1) * width, head_rows(g)] += in2[p, g].astype(F32)
        return carry

    def ready(n):
        for p in range(len(PLANS)):
            hid_wait(p, n)

    def more(n):
        hid_start(0, n, range(7, 0, -1))
        hid_own(0, n).start()

    def attention(g, carry):
        attend(g)
        return carry

    def slot(t, carry):
        @pl.when(t < kv_heads)
        def _():
            finish(t)

        @pl.when(t == 3)
        def _():
            hid_start(0, 1, (2, 3, 6, 7))

        @pl.when(t == 6)
        def _():
            hid_start(0, 1, (4, 5, 1))
            hid_own(0, 1).start()

        @pl.when((t >= 4) & (t < 4 + kv_heads))
        def _():
            pass_on(t - 4)

        @pl.when((t >= 4) & (t < 4 + kv_heads))
        def _():
            pass_far(t - 4)

        @pl.when((t >= 4) & (t < 4 + kv_heads))
        def _():
            @pl.when(t == 4)
            def _():
                ready(0)

            first(t - 4)

        @pl.when((t >= 8) & (t < 8 + kv_heads))
        def _():
            @pl.when(t == 8)
            def _():
                ready(2)

            second(t - 8)

        @pl.when(t == 8)
        def _():
            hid_start(0, 3, (2, 3, 6, 7))

        @pl.when(t == 11)
        def _():
            hid_start(0, 3, (4, 5, 1))
            hid_own(0, 3).start()

        @pl.when((t == 0) | (t == 1) | (t == 2) | (t == 3))
        def _():
            g = 1 * (t == 1).astype(jnp.int32) + 2 * (t == 2).astype(jnp.int32) + 3 * (t == 3).astype(jnp.int32)
            descend(g, 0, group)
            part_start(g, 0)

        @pl.when(t == 12)
        def _():
            ready(1)
            lax.fori_loop(0, kv_heads, aside, 0)
            for p in range(len(PLANS)):
                copy3(p).start()

        return carry

    def keys_sum(g, carry):
        close(g)
        return carry

    lax.fori_loop(0, kv_heads, attention, 0)
    lax.fori_loop(0, 13, slot, 0)
    lax.fori_loop(0, kv_heads, keys_sum, 0)
    ready(3)
    for p in range(len(PLANS)):
        copy3(p).wait_recv()
    lax.fori_loop(0, kv_heads, third, 0)
    lax.fori_loop(0, kv_heads, ending, 0)

    def sent(g, carry):
        for n in range(2):
            @pl.when(c < 2)
            def _():
                kv_far(g, n).wait_send()

            @pl.when(c != 1)
            def _():
                kv_near(g, n).wait_send()

        for step in range(1, window):
            @pl.when(c >= step)
            def _():
                for n in range(2):
                    part_copy(g, n, step, c - step).wait_send()

        for s in range(4):
            fw_copy(g, s).wait_send()
            if s:
                dv_copy(g, s).wait_send()
        for p in range(len(PLANS)):
            copy1(p, g).wait_send()
            copy2(p, g).wait_send()
        return carry

    lax.fori_loop(0, kv_heads, sent, 0)
    for step in range(1, window):
        @pl.when(c + step < n_ctx)
        def _():
            doc_copy(step, c + step).wait_send()

    for p in range(len(PLANS)):
        copy3(p).wait_send()
        for n in range(4):
            for m in range(1, 8):
                hid_copy(p, n, m).wait_send()


def grouped_call(hidden_in, queries, keys, values, output_gradient, document_index):
    tokens, d = hidden_in.shape
    kv_width = keys.shape[1]
    heads = kv_width // HEAD
    width = d // 32
    plans = len(PLANS)
    span = 3 * tokens
    dma = pltpu.SemaphoreType.DMA
    vmem = pl.BlockSpec(memory_space=pltpu.VMEM)
    hbm = pl.BlockSpec(memory_space=pltpu.HBM)
    return pl.pallas_call(
        grouped,
        out_shape=(
            pltpu.VMEM(queries.shape, BF16),
            pltpu.VMEM(keys.shape, BF16),
            pltpu.VMEM(values.shape, BF16),
            pltpu.VMEM((plans * width, kv_width), F32),
        ),
        in_specs=[hbm] * 6,
        out_specs=(vmem,) * 4,
        scratch_shapes=[
            pltpu.VMEM(queries.shape, BF16),
            pltpu.VMEM(queries.shape, BF16),
            pltpu.VMEM(document_index.shape, jnp.int32),
            pltpu.VMEM((plans, 4, 8 * tokens, width), BF16),
            pltpu.VMEM((heads, 3, 2, tokens, HEAD), BF16),
            pltpu.VMEM((3, 8, tokens), jnp.int32),
            pltpu.VMEM((span, 2 * tokens), F32),
            pltpu.VMEM((heads, queries.shape[1] // (2 * heads * HEAD), span, 2 * tokens), F32),
            pltpu.VMEM((span, HEAD), F32),
            pltpu.VMEM((span, HEAD), F32),
            pltpu.VMEM((heads, 2, 3, tokens, HEAD), BF16),
            pltpu.VMEM((heads, 2, 3, tokens, HEAD), BF16),
            pltpu.VMEM((heads * HEAD, 8 * tokens), BF16),
            pltpu.VMEM((plans, heads, HEAD, width), BF16),
            pltpu.VMEM((plans, heads, HEAD, width), BF16),
            pltpu.VMEM((plans, heads, width, HEAD), BF16),
            pltpu.VMEM((plans, heads, width, HEAD), BF16),
            pltpu.VMEM((plans, heads, HEAD, width), BF16),
            pltpu.VMEM((plans, heads, HEAD, width), BF16),
            dma((3,)), dma((heads, 2)), dma((2, 4)), dma((3,)), dma((3,)),
            dma((heads, 2, 2)), dma((heads, 2, 2)), dma((2, 4, 8)), dma((2, 4, 8)),
            dma((heads, 2, 3)), dma((heads, 2, 3)),
            dma((heads, 6)), dma((heads, 6)), dma((heads, 6)), dma((heads, 6)),
            dma((2, heads)), dma((2, heads)), dma((2, heads)), dma((2, heads)), dma((2,)), dma((2,)),
        ],
        compiler_params=pltpu.CompilerParams(
            collective_id=1, has_side_effects=True, vmem_limit_bytes=58 * 1024 * 1024
        ),
    )(hidden_in, queries, keys, values, output_gradient, document_index)


def store(*refs):
    n = (len(refs) - 1) // 2
    sem = refs[-1]
    copies = [
        pltpu.make_async_copy(a, b, sem.at[i])
        for i, (a, b) in enumerate(zip(refs[:n], refs[n:2 * n]))
    ]
    for copy in copies:
        copy.start()
    for copy in copies:
        copy.wait()


def write_out(*arrays):
    return pl.pallas_call(
        store,
        out_shape=tuple(jax.ShapeDtypeStruct(a.shape, a.dtype) for a in arrays),
        in_specs=[pl.BlockSpec(memory_space=pltpu.VMEM)] * len(arrays),
        out_specs=(pl.BlockSpec(memory_space=pltpu.HBM),) * len(arrays),
        scratch_shapes=[pltpu.SemaphoreType.DMA((len(arrays),))],
        compiler_params=pltpu.CompilerParams(vmem_limit_bytes=8 * 1024 * 1024),
    )(*arrays)


def shards(*arrays):
    sizes = (lax.axis_size("dp"), lax.axis_size("ctx"))
    call = grouped_call if sizes == (8, 4) else general_call
    return write_out(*call(*arrays))


def solution(mesh):
    return jax.shard_map(
        shards,
        mesh=mesh,
        in_specs=(P(("dp", "ctx"), None),) * 5 + (P("dp", "ctx"),),
        out_specs=(P(("dp", "ctx"), None),) * 4,
        check_vma=False,
    )
```
